256 devices in a mesh: search: 32 (over x, z), mp: 8 (over y, core).
Axes of the slice: x: 4, y: 4, z: 8, core: 2. Of those that a mesh axis runs over, the one named last changes fastest.
Arguments:
- queries: bfloat16 [512, 2, 128, 192], P('search', None, 'mp'), may hold values from -240 to 240
- new_latents: bfloat16 [512, 2, 576], P('search'), may hold values from -6 to 6
- parent_cache: bfloat16 [32, 4096, 576], P('search'), may hold values from -4 to 4
- parent_of: int32 [512], P('search'), may hold values from 0 to 31, as said below
- up_keys: bfloat16 [128, 128, 512], P('mp'), may hold values from -0.5 to 0.5
- up_values: bfloat16 [128, 512, 128], P('mp'), may hold values from -0.25 to 0.25
- out_proj: bfloat16 [16384, 7168], P('mp', 'search'), may hold values from -0.09375 to 0.09375
- hidden_in: bfloat16 [512, 2, 7168], P('search', None, 'mp'), may hold values from -22 to 22
- router: bfloat16 [7168, 32], P('mp'), may hold values from -0.0625 to 0.0625
- routes: int32 [512, 2, 8], P('search'), may hold values from 0 to 31, all different within a row; in each aligned block of 32 rows (0 to 31, 32 to 63, ..., all dimensions but the last counted through in order) at most 12 rows name the same one
- w_gate: bfloat16 [32, 7168, 1024], P('search', None, 'mp'), may hold values from -0.0625 to 0.0625
- w_up: bfloat16 [32, 7168, 1024], P('search', None, 'mp'), may hold values from -0.0625 to 0.0625
- w_down: bfloat16 [32, 1024, 7168], P('search', 'mp'), may hold values from -0.25 to 0.25
Outputs:
- mixed: bfloat16 [512, 2, 7168], P('search', None, 'mp')
The draws below stay inside these ranges and needn't reach their ends.
Inputs may be any that keep to these rules, and one draw needn't show every extreme that they name: `parent_of`: the children of one device fall into 16 groups of 1 children with a common parent, the groups' parents all different; every parent has 16 children. `routes`: each row names 8 different experts; in the rows of one device no expert is named more than 12 times, and that most is reached.
All inputs are finite; a program needn't handle non-finite values.
Results may differ from the reference program's by a relative error of at most 0.017.
Values may be sent and summed in bfloat16 or wider, within the bound.
No kernel may reach another device: no remote copies, remote signals or barrier semaphores. Data moves between devices by JAX's collectives and lax.ppermute only.
A program may use at most 128 MiB of HBM per device.

```python
import math
import jax
import jax.numpy as jnp
import numpy as np
from jax import lax

D = 7168
HEADS = 128
NOPE = 128
ROPE = 64
LATENT = 512
VDIM = 128
TOPK = 8
EXPERT_HIDDEN = 1024
NEW = 2
C_DEV = 16
PREFIX = 4096
CHILDREN = 512
PARENTS = 32
EXPERTS = 32
GROUPS = 16
KPAIR = 1
CAP = 12
N_SEARCH = 32
N_MP = 8


STRENGTHS = (120.0, 240.0, 380.0)


def parent_table(key):
    base = jax.random.fold_in(key, 101)
    first, second, third, fourth = jax.random.split(base, 4)
    shuffle_a = jax.random.permutation(first, N_SEARCH)
    shuffle_b = jax.random.permutation(second, N_SEARCH)
    offsets = jax.random.permutation(third, N_SEARCH)[:GROUPS]
    orders = jax.vmap(lambda member: jax.random.permutation(member, C_DEV))(jax.random.split(fourth, N_SEARCH))
    group_of = orders // KPAIR
    devices = jnp.arange(N_SEARCH)[:, None]
    target = shuffle_b[(shuffle_a[devices] + offsets[group_of]) % N_SEARCH]
    return target.reshape(CHILDREN).astype(jnp.int32)


def cache_parts(key):
    base = jax.random.fold_in(key, 202)
    first, second, third = jax.random.split(base, 3)
    latent_part = jnp.clip(jax.random.normal(first, (PARENTS, PREFIX, LATENT)), -4.0, 4.0)
    rope_part = jnp.clip(jax.random.normal(second, (PARENTS, PREFIX, ROPE)), -4.0, 4.0)
    anchor = jax.random.randint(third, (PARENTS,), 0, PREFIX - 1)
    strength = jnp.array(STRENGTHS, jnp.float32)[jnp.arange(PARENTS) % 3]
    anchor_key = rope_part[jnp.arange(PARENTS), anchor]
    return (latent_part, rope_part, anchor_key, strength)


def own_rope(key):
    return 1.5 * jnp.clip(jax.random.normal(jax.random.fold_in(key, 303), (CHILDREN, NEW, ROPE)), -4.0, 4.0)


def draw_parent_of(key, part):
    return parent_table(key)


def draw_parent_cache(key, part):
    parts = cache_parts(key)
    return jnp.concatenate([parts[0], parts[1]], axis=-1).astype(jnp.bfloat16)


def draw_new_latents(key, part):
    latent_key = jax.random.fold_in(key, 505)
    latent_part = jnp.clip(jax.random.normal(latent_key, (CHILDREN, NEW, LATENT)), -4.0, 4.0)
    return jnp.concatenate([latent_part, own_rope(key)], axis=-1).astype(jnp.bfloat16)


def draw_queries(key, part):
    base = jax.random.fold_in(key, 404)
    first, second = jax.random.split(base, 2)
    nope_part = jnp.clip(jax.random.normal(first, (CHILDREN, NEW, HEADS, NOPE)), -4.0, 4.0)
    noise = jnp.clip(jax.random.normal(second, (CHILDREN, NEW, HEADS, ROPE)), -4.0, 4.0)
    own_keys = own_rope(key)
    shared = own_keys[:, 0] + own_keys[:, 1]
    rope_part = 0.6 * shared[:, None, None, :] + 0.5 * noise
    return jnp.concatenate([nope_part, rope_part], axis=-1).astype(jnp.bfloat16)


def draw_hidden_in(key, part):
    base = jax.random.fold_in(key, 606)
    first, second = jax.random.split(base, 2)
    row_scale = jnp.exp(jax.random.uniform(second, (CHILDREN, NEW, 1), minval=math.log(0.3), maxval=math.log(3.0)))
    ramp = jnp.arange(D, dtype=jnp.float32) / D
    values = jnp.clip(jax.random.normal(first, (CHILDREN, NEW, D)), -4.0, 4.0)
    column_scale = 3.0 ** ramp / 1.7
    return (values * row_scale * column_scale).astype(jnp.bfloat16)


def raised(values, own_key, source, target, blocks, factor):
    def block_of(dim):
        return (jnp.arange(values.shape[dim]) // (values.shape[dim] // blocks)).reshape((-1,) + (1,) * (values.ndim - 1 - dim))

    first = jax.random.permutation(own_key, blocks)[block_of(target)]
    second = (block_of(target) + blocks // 2) % blocks
    return jnp.where((block_of(source) == first) | (block_of(source) == second), factor * values, values)


def steps_of(key, dims, shards, smallest, high):
    def one(axis_at, shards_of):
        heights = jax.random.uniform(jax.random.fold_in(jax.random.fold_in(key, 6), axis_at), (shards_of,), jnp.float32, smallest / len(shards), high / len(shards))
        return jnp.repeat(jnp.exp(heights), dims[axis_at] // shards_of).reshape((-1,) + (1,) * (len(dims) - axis_at - 1))

    factor_of = one(*shards[0])
    for cut in shards[1:]:
        factor_of = factor_of * one(*cut)
    return factor_of


def assign_block(own_key, own, number, rows, count, top, bound, slope):
    ranking = jax.random.permutation(own_key, count)
    crowded, usual = load_shares(count, rows * top, bound, slope, True), load_shares(count, rows * top, bound, slope, False)
    places = jnp.arange(count)

    def named(tallies, rotation):
        used = int((tallies > 0).sum())
        fixed = max(1, used // 4)
        shifted = fixed + (places - fixed + rotation * (used - fixed)) % max(1, count - fixed)
        return jnp.zeros((count,), jnp.int32).at[ranking[jnp.where(places < fixed, places, shifted)]].set(jnp.asarray(tallies, jnp.int32))

    tallies = jnp.where(number % 4 == 0, named(crowded, number // 4), named(usual, number - number // 4 - 1))
    mixed = jax.random.permutation(jax.random.fold_in(own, 3), count)
    giver, receiver = mixed[0:count // 2 * 2:2], mixed[1:count // 2 * 2:2]
    slack = jnp.minimum(tallies[giver] - 1, bound - tallies[receiver]) // 2
    slack = jnp.where((giver == ranking[0]) | (receiver == ranking[0]) | (tallies[receiver] == 0), 0, jnp.maximum(slack, 0))
    shifted = jax.random.randint(jax.random.fold_in(own, 4), (count // 2,), 0, 1 << 20) % (slack + 1)
    tallies = tallies.at[giver].add(-shifted).at[receiver].add(shifted)
    items = jnp.searchsorted(jnp.cumsum(tallies), jnp.arange(rows * top), side="right").astype(jnp.int32)
    grid = items.reshape(top, rows).T
    grid = grid[jax.random.permutation(jax.random.fold_in(own, 1), rows)]
    rotation = jax.random.randint(jax.random.fold_in(own, 2), (rows, 1), 0, top)
    return jnp.take_along_axis(grid, (jnp.arange(top)[None, :] + rotation) % top, axis=1)


def load_shares(count, total, limit, lean, full):
    portions = [(1 << 20) // math.isqrt(standing ** lean) + 1 for standing in range(1, count + 1)]
    largest = limit if full else min(limit, max(-(-total // count), total * portions[0] // sum(portions)))
    least = 1 if total - largest >= count - 1 else 0
    counts, spare = [largest] + [least] * (count - 1), total - largest - least * (count - 1)
    while spare > 0:
        candidates = [i for i in range(1, count) if counts[i] < largest] or [i for i in range(1, count) if counts[i] < limit]
        whole, remaining = sum([portions[i] for i in candidates]), spare
        for i in candidates:
            more = min(limit - counts[i], max(1, remaining * portions[i] // whole), spare)
            counts[i] = counts[i] + more
            spare = spare - more
    return np.array(counts)


def normal_values(stream_key, shape, spread, bound, cuts=(), kind=jnp.bfloat16):
    loudness = steps_of(stream_key, shape, cuts, -0.22, 0.18) if cuts else 1.0
    values = jax.random.normal(stream_key, shape, jnp.float32) * spread * loudness
    return jnp.minimum(jnp.maximum(values, -bound), bound).astype(kind)


def noise_with(key, extent, width, most, shards, heavy, kind=jnp.bfloat16):
    drawn = width * jax.random.normal(key, extent, jnp.float32)
    if shards:
        drawn = drawn * steps_of(key, extent, shards, -0.22, 0.18)
    return jnp.clip(raised(drawn, jax.random.fold_in(key, 3), *heavy), -most, most).astype(kind)


def setup_inputs(seed: int = 0) -> dict:
    key_list = jax.random.split(jax.random.key(seed), 14)
    queries = draw_queries(jax.random.fold_in(key_list[13], 71), 0)
    new_latents = draw_new_latents(jax.random.fold_in(key_list[13], 71), 0)
    parent_cache = draw_parent_cache(jax.random.fold_in(key_list[13], 71), 0)
    parent_of = draw_parent_of(jax.random.fold_in(key_list[13], 71), 0)
    up_keys = normal_values(key_list[4], (HEADS, NOPE, LATENT), NOPE ** -0.5, 0.5, ((0, 8),))
    up_values = normal_values(key_list[5], (HEADS, LATENT, VDIM), LATENT ** -0.5, 0.25, ((0, 8),))
    out_proj = noise_with(key_list[6], (HEADS * VDIM, D), (HEADS * VDIM) ** -0.5, 0.09375, ((0, 8), (1, 32)), (0, 1, 32, 2.75))
    hidden_in = draw_hidden_in(jax.random.fold_in(key_list[13], 71), 0)
    router = normal_values(key_list[8], (D, EXPERTS), D ** -0.5, 0.0625, ((0, 8),))
    routes_keys = jax.random.split(jax.random.fold_in(key_list[9], 1), CHILDREN * NEW // (C_DEV * NEW))
    routes_turns = jax.random.permutation(jax.random.fold_in(key_list[9], 3), CHILDREN * NEW // (C_DEV * NEW))
    routes = jax.vmap(lambda own, number: assign_block(jax.random.fold_in(key_list[9], 2), own, number, C_DEV * NEW, EXPERTS, TOPK, CAP, 2))(routes_keys, routes_turns).reshape((CHILDREN, NEW, TOPK))
    w_gate = normal_values(key_list[10], (EXPERTS, D, EXPERT_HIDDEN), D ** -0.5, 0.0625, ((0, 32), (2, 8)))
    w_up = normal_values(key_list[11], (EXPERTS, D, EXPERT_HIDDEN), D ** -0.5, 0.0625, ((0, 32), (2, 8)))
    w_down = noise_with(key_list[12], (EXPERTS, EXPERT_HIDDEN, D), EXPERT_HIDDEN ** -0.5, 0.25, ((0, 32), (1, 8)), (1, 2, 8, 2.0))
    return {"queries": queries, "new_latents": new_latents, "parent_cache": parent_cache, "parent_of": parent_of, "up_keys": up_keys, "up_values": up_values, "out_proj": out_proj, "hidden_in": hidden_in, "router": router, "routes": routes, "w_gate": w_gate, "w_up": w_up, "w_down": w_down}


def attend_child(query_block, own_keys, prefix_cache, up_keys, up_values):
    softmax_scale = (NOPE + ROPE) ** (-0.5)
    latent_query = jnp.einsum('thn,hnl->thl', query_block[..., :NOPE].astype(jnp.float32), up_keys.astype(jnp.float32)).astype(jnp.bfloat16)
    full_query = jnp.concatenate([latent_query, query_block[..., NOPE:]], axis=-1)
    all_keys = jnp.concatenate([prefix_cache, own_keys], axis=0)
    scores = jnp.dot(full_query.reshape(NEW * HEADS, LATENT + ROPE), all_keys.T, preferred_element_type=jnp.float32) * softmax_scale
    scores = scores.reshape(NEW, HEADS, PREFIX + NEW)
    token_pos = jnp.arange(NEW, dtype=jnp.int32)[:, None]
    key_pos = jnp.arange(PREFIX + NEW, dtype=jnp.int32)[None, :]
    visible = key_pos < PREFIX + token_pos + 1
    scores = jnp.where(visible[:, None, :], scores, -jnp.inf)
    row_peak = lax.optimization_barrier(jnp.max(scores, axis=-1, keepdims=True))
    weights = jnp.exp(scores - row_peak)
    row_mass = lax.optimization_barrier(jnp.sum(weights, axis=-1, keepdims=True))
    summed = jnp.dot(weights.astype(jnp.bfloat16).reshape(NEW * HEADS, PREFIX + NEW), all_keys[:, :LATENT], preferred_element_type=jnp.float32)
    latent_out = (summed.reshape(NEW, HEADS, LATENT) / row_mass).astype(jnp.bfloat16)
    head_out = jnp.einsum('thl,hlv->thv', latent_out.astype(jnp.float32), up_values.astype(jnp.float32)).astype(jnp.bfloat16)
    return head_out.reshape(NEW, HEADS * VDIM)

def reference(queries, new_latents, parent_cache, parent_of, up_keys, up_values, out_proj, hidden_in, router, routes, w_gate, w_up, w_down):

    def one_child(child_index):
        prefix_cache = parent_cache[parent_of[child_index]]
        return attend_child(queries[child_index], new_latents[child_index], prefix_cache, up_keys, up_values)
    attention = lax.map(one_child, jnp.arange(CHILDREN, dtype=jnp.int32))
    token_count = CHILDREN * NEW
    attention = attention.reshape(token_count, HEADS * VDIM)
    residual = (hidden_in.reshape(token_count, D).astype(jnp.float32) + jnp.dot(attention, out_proj, preferred_element_type=jnp.float32)).astype(jnp.bfloat16)
    residual_wide = residual.astype(jnp.float32)
    inv_rms = lax.rsqrt(lax.optimization_barrier(jnp.mean(residual_wide * residual_wide, axis=1)) + 1e-06)
    logits = jnp.dot(residual, router, preferred_element_type=jnp.float32) * inv_rms[:, None]
    normed = (residual_wide * inv_rms[:, None]).astype(jnp.bfloat16)
    picked = routes.reshape(token_count, TOPK)
    affinity = jax.nn.sigmoid(logits)
    chosen = jnp.take_along_axis(affinity, picked, axis=1)
    gate_weights = 2.5 * chosen / lax.optimization_barrier(jnp.sum(chosen, axis=1, keepdims=True))
    part_width = EXPERT_HIDDEN // N_MP
    slot_limit = N_SEARCH * CAP

    def one_expert(expert_mix, expert):
        matches = picked == expert
        weight_row = lax.optimization_barrier(jnp.sum(jnp.where(matches, gate_weights, 0.0), axis=1))
        selected = jnp.any(matches, axis=1)
        row_index = jnp.nonzero(selected, size=slot_limit, fill_value=0)[0]
        live_slot = jnp.arange(slot_limit) < jnp.sum(selected)
        inputs = normed[row_index]
        gate_act = jnp.dot(inputs, w_gate[expert], preferred_element_type=jnp.float32)
        up_act = jnp.dot(inputs, w_up[expert], preferred_element_type=jnp.float32)
        expert_hidden = (jax.nn.silu(gate_act) * up_act).astype(jnp.bfloat16)
        partials = jnp.einsum('smk,mkd->msd', expert_hidden.reshape(slot_limit, N_MP, part_width).astype(jnp.float32), w_down[expert].reshape(N_MP, part_width, D).astype(jnp.float32)).astype(jnp.bfloat16)
        expert_out = lax.optimization_barrier(jnp.sum(partials.astype(jnp.float32), axis=0))
        row_scale = jnp.where(live_slot, weight_row[row_index], 0.0)
        return (expert_mix.at[row_index].add(expert_out * row_scale[:, None]), None)
    expert_mix, unused = lax.scan(one_expert, jnp.zeros((token_count, D), jnp.float32), jnp.arange(EXPERTS, dtype=jnp.int32))
    mixed = (residual_wide + expert_mix).astype(jnp.bfloat16)
    return mixed.reshape(CHILDREN, NEW, D)
```

```python
import jax
import jax.numpy as jnp
from jax import lax
from jax.sharding import Mesh
from jax.sharding import PartitionSpec as P

D = 7168
SEARCH = ("x", "z")
MP = ("y", "c")
BF16 = jnp.bfloat16
F32 = jnp.float32


def exchange(values, axes):
    return lax.all_to_all(values, axes, split_axis=0, concat_axis=0, tiled=True)


def to_other_core(values):
    return lax.ppermute(values, "c", [(0, 1), (1, 0)])


def select_rows(matrix, rows):
    return jnp.dot(matrix, rows, preferred_element_type=F32).astype(BF16)


def attend(nope, rope, own_keys, prefix, up_keys, up_values):
    heads, rows, _ = nope.shape
    children, steps, kv_width = own_keys.shape
    latent_width = up_keys.shape[2]
    scale = float(nope.shape[2] + rope.shape[2]) ** (-0.5)
    latent_query = jnp.einsum("hrn,hnl->hrl", nope, up_keys, preferred_element_type=F32).astype(BF16)
    query = jnp.concatenate([latent_query, rope], axis=-1)
    scores = (
        lax.dot_general(
            query.reshape(heads * rows, kv_width),
            prefix,
            (((1,), (1,)), ((), ())),
            preferred_element_type=F32,
        )
        * scale
    )
    by_child = query.reshape(heads, children, steps, kv_width)
    own = jnp.einsum("hctk,cuk->hctu", by_child, own_keys, preferred_element_type=F32) * scale
    causal = jnp.arange(steps)[None, :] <= jnp.arange(steps)[:, None]
    own = jnp.where(causal, own, -jnp.inf)
    peak = jnp.maximum(jnp.max(scores, axis=1), jnp.max(own, axis=-1).reshape(-1))
    weights = jnp.exp(scores - peak[:, None])
    own_weights = jnp.exp(own - peak.reshape(heads, children, steps)[..., None])
    mass = jnp.sum(weights, axis=1) + jnp.sum(own_weights, axis=-1).reshape(-1)
    summed = jnp.dot(weights.astype(BF16), prefix[:, :latent_width], preferred_element_type=F32)
    own_sum = jnp.sum(
        own_weights[..., None] * own_keys[None, :, None, :, :latent_width].astype(F32), axis=3
    )
    latent_out = ((summed + own_sum.reshape(heads * rows, latent_width)) / mass[:, None]).astype(BF16)
    return jnp.einsum(
        "hrl,hlv->hrv",
        latent_out.reshape(heads, rows, latent_width),
        up_values,
        preferred_element_type=F32,
    ).astype(BF16)


def local(
    queries,
    new_latents,
    parent_cache,
    parent_of,
    up_keys,
    up_values,
    out_proj,
    hidden_in,
    router,
    routes,
    w_gate,
    w_up,
    w_down,
):
    n_x, n_z, n_y, n_c = (lax.axis_size(a) for a in ("x", "z", "y", "c"))
    searchers = n_x * n_z
    children, steps, heads, query_width = queries.shape
    nope_width, latent_width = up_keys.shape[1:]
    rope_width = query_width - nope_width
    kv_width = parent_cache.shape[2]
    value_width = up_values.shape[2]
    tokens = children * steps
    width = hidden_in.shape[2]
    block = out_proj.shape[1]
    core = lax.axis_index("c")

    proj = lax.all_gather(out_proj, "x", axis=0, tiled=False)
    gate_up = jnp.concatenate(
        [w_gate[0].reshape(n_y, D // n_y, -1), w_up[0].reshape(n_y, D // n_y, -1)], axis=-1
    )
    gate_up = exchange(gate_up, "y")
    hidden_here = w_down.shape[1]
    down = exchange(w_down[0].reshape(hidden_here, n_y * n_c, width).transpose(1, 0, 2), MP)

    placer = (jnp.arange(searchers, dtype=jnp.int32)[:, None] == parent_of[None, :]).astype(BF16)
    nope = queries[..., :nope_width].transpose(0, 2, 1, 3).reshape(children, -1)
    rope = queries[..., nope_width:].transpose(0, 2, 1, 3).reshape(children, -1)
    keys = new_latents.reshape(children, -1)
    mark = jnp.ones((children, 128), BF16)
    payload = select_rows(placer, jnp.concatenate([nope, rope, keys, mark], axis=1))
    arrived = exchange(payload.reshape(searchers, 1, -1), SEARCH).reshape(searchers, -1)

    n0, n1, n2 = nope.shape[1], rope.shape[1], keys.shape[1]
    present = arrived[:, n0 + n1 + n2].astype(F32)
    span = jnp.arange(searchers, dtype=jnp.int32)
    before = jnp.sum(jnp.where(span[None, :] < span[:, None], present[None, :], 0.0), axis=1)
    chosen = (
        (jnp.arange(children, dtype=F32)[:, None] == before[None, :]) & (present[None, :] > 0)
    ).astype(BF16)
    packed = select_rows(chosen, arrived)
    homes = jnp.sum(chosen.astype(F32) * span.astype(F32)[None, :], axis=1)

    def by_head(flat, size):
        return flat.reshape(children, heads, steps, size).transpose(1, 0, 2, 3).reshape(heads, tokens, size)

    head_out = attend(
        by_head(packed[:, :n0], nope_width),
        by_head(packed[:, n0 : n0 + n1], rope_width),
        packed[:, n0 + n1 : n0 + n1 + n2].reshape(children, steps, kv_width),
        parent_cache[0],
        up_keys,
        up_values,
    )

    attention = head_out.transpose(1, 0, 2).reshape(tokens, heads * value_width)
    half = attention.shape[1] // 2
    home_rows = jnp.broadcast_to(jnp.repeat(homes, steps)[:, None], (tokens, 128)).astype(BF16)
    first = lax.all_gather(attention[:, :half], "z", axis=0, tiled=False)
    second = lax.all_gather(
        jnp.concatenate([attention[:, half:], home_rows], axis=1), "z", axis=0, tiled=False
    )
    all_homes = second[:, ::steps, half].astype(jnp.int32)
    gathered = jnp.concatenate([first, second[:, :, :half]], axis=2).reshape(n_z * tokens, -1)
    partial = jnp.einsum("rk,xkf->xrf", gathered, proj, preferred_element_type=F32).astype(BF16)

    rows_half = n_z * tokens // n_c
    pieces = exchange(partial.reshape(n_y * n_c, rows_half, block), MP)
    summed = jnp.sum(pieces.astype(F32), axis=0).astype(BF16)

    zs = n_z // n_c
    my_homes = lax.dynamic_slice_in_dim(all_homes, core * zs, zs, axis=0)
    scatter = (span[None, :, None] == my_homes[:, None, :]).astype(BF16)
    slots = jnp.einsum(
        "zsj,zjf->szf",
        scatter,
        summed.reshape(zs, children, steps * block),
        preferred_element_type=F32,
    ).astype(BF16)
    landed = exchange(slots.reshape(searchers, zs * steps, block), SEARCH)
    landed = landed.reshape(n_x, n_z, zs, steps, block).transpose(0, 2, 3, 1, 4)
    parent_slot = (
        (jnp.arange(n_x, dtype=jnp.int32)[:, None] * n_z + core * zs)
        + jnp.arange(zs, dtype=jnp.int32)[None, :]
    ).reshape(-1)
    picker = (parent_of[:, None] == parent_slot[None, :]).astype(BF16)
    mine = select_rows(picker, landed.reshape(n_x * zs, -1)).reshape(tokens, n_c, width)
    keep = jnp.where(core == 0, mine[:, 0], mine[:, 1])
    give = jnp.where(core == 0, mine[:, 1], mine[:, 0])
    projected = keep.astype(F32) + to_other_core(give).astype(F32)
    residual = (hidden_in.reshape(tokens, width).astype(F32) + projected).astype(BF16)
    residual_wide = residual.astype(F32)

    experts = router.shape[1]
    topk = routes.shape[2]
    capacity = min(tokens, 3 * tokens * topk // (2 * experts))
    picked = routes.reshape(tokens, topk)
    named = jnp.any(
        picked[None, :, :] == jnp.arange(experts, dtype=jnp.int32)[:, None, None], axis=2
    )
    earlier = (
        jnp.arange(tokens, dtype=jnp.int32)[:, None] < jnp.arange(tokens, dtype=jnp.int32)[None, :]
    )
    rank = jnp.dot(named.astype(BF16), earlier.astype(BF16), preferred_element_type=F32)
    slot_of = (
        named[:, None, :]
        & (rank[:, None, :] == jnp.arange(capacity, dtype=F32)[None, :, None])
    ).reshape(experts * capacity, tokens)
    outgoing = select_rows(slot_of.astype(BF16), residual)
    rows = exchange(outgoing.reshape(experts, capacity, width), SEARCH).reshape(
        experts * capacity, width
    )

    squares = jnp.sum(residual_wide * residual_wide, axis=1, keepdims=True)
    router_part = jnp.dot(residual, router, preferred_element_type=F32)
    stats = jnp.concatenate(
        [router_part, squares, jnp.zeros((tokens, 128 - experts - 1), F32)], axis=1
    )
    stats = exchange(jnp.broadcast_to(stats[None], (n_y * n_c,) + stats.shape), MP)
    stats = jnp.sum(stats, axis=0)
    home_rms = lax.rsqrt(stats[:, experts] / D + 1e-06)
    affinity = jax.nn.sigmoid(stats[:, :experts] * home_rms[:, None])
    chosen_affinity = jnp.where(named.T, affinity, 0.0)
    gate_weight = 2.5 * chosen_affinity / jnp.sum(chosen_affinity, axis=1, keepdims=True)

    other = to_other_core(rows)
    low = jnp.where(core == 0, rows, other)
    high = jnp.where(core == 0, other, rows)
    both = jnp.concatenate([low, high], axis=1)
    both_wide = both.astype(F32)
    row_squares = jnp.sum(both_wide * both_wide, axis=1).reshape(1, -1, 128)
    row_squares = exchange(jnp.broadcast_to(row_squares, (n_y,) + row_squares.shape[1:]), "y")
    row_rms = lax.rsqrt(jnp.sum(row_squares, axis=0).reshape(-1) / D + 1e-06)
    acts = jnp.einsum("rk,ykn->yrn", both, gate_up, preferred_element_type=F32).astype(BF16)
    acts = jnp.sum(exchange(acts, "y").astype(F32), axis=0) * row_rms[:, None]
    hidden = (jax.nn.silu(acts[:, :hidden_here]) * acts[:, hidden_here:]).astype(BF16)
    all_hidden = lax.all_gather(hidden, MP, axis=1, tiled=True)
    expert_out = jnp.dot(
        all_hidden, down.reshape(-1, width), preferred_element_type=F32
    ).astype(BF16)
    returned = exchange(expert_out.reshape(experts, capacity, width), SEARCH).reshape(
        experts * capacity, width
    )

    weight_of = jnp.where(
        slot_of.reshape(experts, capacity, tokens), gate_weight.T[:, None, :], 0.0
    ).reshape(experts * capacity, tokens)
    upper = weight_of.astype(BF16)
    lower = (weight_of - upper.astype(F32)).astype(BF16)
    dims = (((0,), (0,)), ((), ()))
    expert_mix = lax.dot_general(
        upper, returned, dims, preferred_element_type=F32
    ) + lax.dot_general(lower, returned, dims, preferred_element_type=F32)
    mixed = (residual_wide + expert_mix).astype(BF16)
    return mixed.reshape(children, steps, width)


def solution(mesh):
    fine = Mesh(mesh.devices.reshape(4, 8, 4, 2), ("x", "z", "y", "c"))
    in_specs = (
        P(SEARCH, None, MP, None),
        P(SEARCH, None, None),
        P(SEARCH, None, None),
        P(SEARCH),
        P(MP, None, None),
        P(MP, None, None),
        P(MP, SEARCH),
        P(SEARCH, None, MP),
        P(MP, None),
        P(SEARCH, None, None),
        P(SEARCH, None, MP),
        P(SEARCH, None, MP),
        P(SEARCH, MP, None),
    )
    out_specs = P(SEARCH, None, MP)
    return jax.shard_map(local, mesh=fine, in_specs=in_specs, out_specs=out_specs, check_vma=False)
```

```python
import jax
import jax.numpy as jnp
from jax import lax
from jax.experimental.layout import Layout, with_layout_constraint
from jax.sharding import Mesh
from jax.sharding import PartitionSpec as P

D = 7168
SEARCH = ("x", "z")
MP = ("y", "c")
BF16 = jnp.bfloat16
F32 = jnp.float32


def exchange(values, axes):
    return lax.all_to_all(values, axes, split_axis=0, concat_axis=0, tiled=True)


def to_other_core(values):
    return lax.ppermute(values, "c", [(0, 1), (1, 0)])


def along_y(values, step):
    if step == 0:
        return values
    n = lax.axis_size("y")
    return lax.ppermute(values, "y", [(i, (i + step) % n) for i in range(n)])


def row_major(values):
    return with_layout_constraint(values, Layout(major_to_minor=tuple(range(values.ndim))))


def select_rows(matrix, rows):
    return jnp.dot(matrix, rows, preferred_element_type=F32).astype(BF16)


def attend(nope, rope, own_keys, prefix, up_keys, up_values):
    heads, rows, _ = nope.shape
    children, steps, kv_width = own_keys.shape
    latent_width = up_keys.shape[2]
    scale = float(nope.shape[2] + rope.shape[2]) ** (-0.5)
    latent_query = jnp.einsum("hrn,hnl->hrl", nope, up_keys, preferred_element_type=F32).astype(BF16)
    query = jnp.concatenate([latent_query, rope], axis=-1)
    scores = (
        lax.dot_general(
            query.reshape(heads * rows, kv_width),
            prefix,
            (((1,), (1,)), ((), ())),
            preferred_element_type=F32,
        )
        * scale
    )
    by_child = query.reshape(heads, children, steps, kv_width)
    own = jnp.einsum("hctk,cuk->hctu", by_child, own_keys, preferred_element_type=F32) * scale
    causal = jnp.arange(steps)[None, :] <= jnp.arange(steps)[:, None]
    own = jnp.where(causal, own, -jnp.inf)
    peak = jnp.maximum(jnp.max(scores, axis=1), jnp.max(own, axis=-1).reshape(-1))
    weights = jnp.exp(scores - peak[:, None])
    own_weights = jnp.exp(own - peak.reshape(heads, children, steps)[..., None])
    mass = jnp.sum(weights, axis=1) + jnp.sum(own_weights, axis=-1).reshape(-1)
    summed = jnp.dot(weights.astype(BF16), prefix[:, :latent_width], preferred_element_type=F32)
    own_sum = jnp.sum(
        own_weights[..., None] * own_keys[None, :, None, :, :latent_width].astype(F32), axis=3
    )
    latent_out = ((summed + own_sum.reshape(heads * rows, latent_width)) / mass[:, None]).astype(BF16)
    return jnp.einsum(
        "hrl,hlv->hrv",
        latent_out.reshape(heads, rows, latent_width),
        up_values,
        preferred_element_type=F32,
    ).astype(BF16)


def local(
    queries,
    new_latents,
    parent_cache,
    parent_of,
    up_keys,
    up_values,
    out_proj,
    hidden_in,
    router,
    routes,
    w_gate,
    w_up,
    w_down,
):
    n_x, n_z, n_y, n_c = (lax.axis_size(a) for a in ("x", "z", "y", "c"))
    searchers = n_x * n_z
    children, steps, heads, query_width = queries.shape
    nope_width, latent_width = up_keys.shape[1:]
    rope_width = query_width - nope_width
    kv_width = parent_cache.shape[2]
    value_width = up_values.shape[2]
    tokens = children * steps
    width = hidden_in.shape[2]
    block = out_proj.shape[1]
    core = lax.axis_index("c")

    proj = lax.all_gather(out_proj, "x", axis=0, tiled=False)
    hidden_here = w_down.shape[1]
    here = lax.axis_index("y")
    gate_up, down = [], []
    for k in range(n_y):
        to = lax.rem(here + k, n_y)
        gate_k = lax.dynamic_slice_in_dim(w_gate[0], to * (D // n_y), D // n_y, axis=0)
        up_k = lax.dynamic_slice_in_dim(w_up[0], to * (D // n_y), D // n_y, axis=0)
        gate_up.append(along_y(row_major(jnp.concatenate([gate_k, up_k], axis=1)), k))
        down_k = lax.dynamic_slice_in_dim(w_down[0], to * (D // n_y), D // n_y, axis=1)
        down.append(along_y(row_major(down_k), k))
    down = jnp.concatenate(down, axis=0)
    down_here = lax.dynamic_slice_in_dim(down, core * width, width, axis=1)
    down_there = to_other_core(
        row_major(lax.dynamic_slice_in_dim(down, (1 - core) * width, width, axis=1))
    )

    placer = (jnp.arange(searchers, dtype=jnp.int32)[:, None] == parent_of[None, :]).astype(BF16)
    nope = queries[..., :nope_width].transpose(0, 2, 1, 3).reshape(children, -1)
    rope = queries[..., nope_width:].transpose(0, 2, 1, 3).reshape(children, -1)
    keys = new_latents.reshape(children, -1)
    mark = jnp.ones((children, 128), BF16)
    payload = select_rows(placer, jnp.concatenate([nope, rope, keys, mark], axis=1))
    arrived = exchange(payload.reshape(searchers, 1, -1), SEARCH).reshape(searchers, -1)

    n0, n1, n2 = nope.shape[1], rope.shape[1], keys.shape[1]
    present = arrived[:, n0 + n1 + n2].astype(F32)
    span = jnp.arange(searchers, dtype=jnp.int32)
    before = jnp.sum(jnp.where(span[None, :] < span[:, None], present[None, :], 0.0), axis=1)
    chosen = (
        (jnp.arange(children, dtype=F32)[:, None] == before[None, :]) & (present[None, :] > 0)
    ).astype(BF16)
    packed = select_rows(chosen, arrived)
    homes = jnp.sum(chosen.astype(F32) * span.astype(F32)[None, :], axis=1)

    def by_head(flat, size):
        return flat.reshape(children, heads, steps, size).transpose(1, 0, 2, 3).reshape(heads, tokens, size)

    nope_rows = by_head(packed[:, :n0], nope_width)
    rope_rows = by_head(packed[:, n0 : n0 + n1], rope_width)
    own_keys = packed[:, n0 + n1 : n0 + n1 + n2].reshape(children, steps, kv_width)
    home_rows = jnp.broadcast_to(jnp.repeat(homes, steps)[:, None], (tokens, 128)).astype(BF16)

    gathered = []
    chunk = heads // 2
    for first in range(0, heads, chunk):
        part = slice(first, first + chunk)
        head_out = attend(
            nope_rows[part], rope_rows[part], own_keys, parent_cache[0], up_keys[part], up_values[part]
        )
        attention = head_out.transpose(1, 0, 2).reshape(tokens, chunk * value_width)
        if first == 0:
            attention = jnp.concatenate([attention, home_rows], axis=1)
            attention, gate_up = lax.optimization_barrier((attention, gate_up))
        else:
            attention, down_here, down_there = lax.optimization_barrier(
                (attention, down_here, down_there)
            )
        gathered.append(exchange(jnp.broadcast_to(attention[None], (n_z,) + attention.shape), "z"))
    all_homes = gathered[0][:, ::steps, chunk * value_width].astype(jnp.int32)
    gathered = jnp.concatenate(
        [g[:, :, : chunk * value_width].reshape(n_z * tokens, -1) for g in gathered], axis=1
    )
    partial = jnp.einsum("rk,xkf->xrf", gathered, proj, preferred_element_type=F32).astype(BF16)

    rows_half = n_z * tokens // n_c
    pieces = exchange(partial.reshape(n_y * n_c, rows_half, block), MP)
    summed = jnp.sum(pieces.astype(F32), axis=0).astype(BF16)

    zs = n_z // n_c
    my_homes = lax.dynamic_slice_in_dim(all_homes, core * zs, zs, axis=0)
    scatter = (span[None, :, None] == my_homes[:, None, :]).astype(BF16)
    slots = jnp.einsum(
        "zsj,zjf->szf",
        scatter,
        summed.reshape(zs, children, steps * block),
        preferred_element_type=F32,
    ).astype(BF16)
    landed = exchange(slots.reshape(searchers, zs * steps, block), SEARCH)
    landed = landed.reshape(n_x, n_z, zs, steps, block).transpose(0, 2, 3, 1, 4)
    parent_slot = (
        (jnp.arange(n_x, dtype=jnp.int32)[:, None] * n_z + core * zs)
        + jnp.arange(zs, dtype=jnp.int32)[None, :]
    ).reshape(-1)
    picker = (parent_of[:, None] == parent_slot[None, :]).astype(BF16)
    mine = select_rows(picker, landed.reshape(n_x * zs, -1)).reshape(tokens, n_c, width)
    keep = jnp.where(core == 0, mine[:, 0], mine[:, 1])
    give = jnp.where(core == 0, mine[:, 1], mine[:, 0])
    projected = keep.astype(F32) + to_other_core(give).astype(F32)
    residual = (hidden_in.reshape(tokens, width).astype(F32) + projected).astype(BF16)
    residual_wide = residual.astype(F32)

    experts = router.shape[1]
    topk = routes.shape[2]
    capacity = min(tokens, 3 * tokens * topk // (2 * experts))
    picked = routes.reshape(tokens, topk)
    named = jnp.any(
        picked[None, :, :] == jnp.arange(experts, dtype=jnp.int32)[:, None, None], axis=2
    )
    earlier = (
        jnp.arange(tokens, dtype=jnp.int32)[:, None] < jnp.arange(tokens, dtype=jnp.int32)[None, :]
    )
    rank = jnp.dot(named.astype(BF16), earlier.astype(BF16), preferred_element_type=F32)
    slot_of = (
        named[:, None, :]
        & (rank[:, None, :] == jnp.arange(capacity, dtype=F32)[None, :, None])
    ).reshape(experts * capacity, tokens)
    outgoing = select_rows(slot_of.astype(BF16), residual)
    quads = capacity // 4
    rows = exchange(outgoing.reshape(experts, quads, 4, width), SEARCH).reshape(
        experts * capacity, width
    )

    squares = jnp.sum(residual_wide * residual_wide, axis=1, keepdims=True)
    router_part = jnp.dot(residual, router, preferred_element_type=F32)
    stats = jnp.concatenate(
        [router_part, squares, jnp.zeros((tokens, 128 - experts - 1), F32)], axis=1
    )
    stats = exchange(jnp.broadcast_to(stats[None], (n_y * n_c,) + stats.shape), MP)
    stats = jnp.sum(stats, axis=0)
    home_rms = lax.rsqrt(stats[:, experts] / D + 1e-06)
    affinity = jax.nn.sigmoid(stats[:, :experts] * home_rms[:, None])
    chosen_affinity = jnp.where(named.T, affinity, 0.0)
    gate_weight = 2.5 * chosen_affinity / jnp.sum(chosen_affinity, axis=1, keepdims=True)

    other = to_other_core(rows)
    low = jnp.where(core == 0, rows, other)
    high = jnp.where(core == 0, other, rows)
    both = jnp.concatenate([low, high], axis=1)
    both_wide = both.astype(F32)
    row_squares = jnp.sum(both_wide * both_wide, axis=1).reshape(-1, 128)
    squares_top = row_squares.astype(BF16)
    squares_rest = (row_squares - squares_top.astype(F32)).astype(BF16)
    ride = jnp.concatenate([squares_top, squares_rest], axis=1)
    lines = ride.shape[0]
    ride = jnp.pad(ride, ((0, -lines % 16), (0, 0)))
    slots_total = experts * capacity
    arrivals = []
    for k in range(1, n_y):
        act = jnp.dot(both, gate_up[k], preferred_element_type=F32).astype(BF16)
        arrivals.append(along_y(jnp.concatenate([act, ride], axis=0), n_y - k).astype(F32))
    acts = jnp.dot(both, gate_up[0], preferred_element_type=F32)
    for arrival in arrivals:
        acts = acts + arrival[:slots_total]
        row_squares = row_squares + (
            arrival[slots_total : slots_total + lines, :128]
            + arrival[slots_total : slots_total + lines, 128:]
        )
    row_rms = lax.rsqrt(row_squares.reshape(-1) / D + 1e-06)
    acts = acts * row_rms[:, None]
    hidden = (jax.nn.silu(acts[:, :hidden_here]) * acts[:, hidden_here:]).astype(BF16)
    hidden_core = jnp.concatenate([along_y(hidden, k) for k in range(n_y)], axis=1)
    hidden_other = to_other_core(hidden_core)
    expert_out = (
        jnp.dot(hidden_core, down_here, preferred_element_type=F32)
        + jnp.dot(hidden_other, down_there, preferred_element_type=F32)
    ).astype(BF16)
    returned = exchange(expert_out.reshape(experts, quads, 4, width), SEARCH).reshape(
        experts * capacity, width
    )

    weight_of = jnp.where(
        slot_of.reshape(experts, capacity, tokens), gate_weight.T[:, None, :], 0.0
    ).reshape(experts * capacity, tokens)
    upper = weight_of.astype(BF16)
    lower = (weight_of - upper.astype(F32)).astype(BF16)
    dims = (((0,), (0,)), ((), ()))
    expert_mix = lax.dot_general(
        upper, returned, dims, preferred_element_type=F32
    ) + lax.dot_general(lower, returned, dims, preferred_element_type=F32)
    mixed = (residual_wide + expert_mix).astype(BF16)
    return mixed.reshape(children, steps, width)


def solution(mesh):
    fine = Mesh(mesh.devices.reshape(4, 8, 4, 2), ("x", "z", "y", "c"))
    in_specs = (
        P(SEARCH, None, MP, None),
        P(SEARCH, None, None),
        P(SEARCH, None, None),
        P(SEARCH),
        P(MP, None, None),
        P(MP, None, None),
        P(MP, SEARCH),
        P(SEARCH, None, MP),
        P(MP, None),
        P(SEARCH, None, None),
        P(SEARCH, None, MP),
        P(SEARCH, None, MP),
        P(SEARCH, MP, None),
    )
    out_specs = P(SEARCH, None, MP)
    return jax.shard_map(local, mesh=fine, in_specs=in_specs, out_specs=out_specs, check_vma=False)
```

```python
import functools

import jax
import jax.numpy as jnp
from jax import lax
from jax.experimental import pallas as pl
from jax.experimental.layout import Layout, with_layout_constraint
from jax.experimental.pallas import tpu as pltpu
from jax.sharding import Mesh
from jax.sharding import PartitionSpec as P

D = 7168
SEARCH = ("x", "z")
MP = ("y", "c")
BF16 = jnp.bfloat16
F32 = jnp.float32


def exchange(values, axes):
    return lax.all_to_all(values, axes, split_axis=0, concat_axis=0, tiled=True)


def to_other_core(values):
    return lax.ppermute(values, "c", [(0, 1), (1, 0)])


def along_y(values, step):
    if step == 0:
        return values
    n = lax.axis_size("y")
    return lax.ppermute(values, "y", [(i, (i + step) % n) for i in range(n)])


def row_major(values):
    return with_layout_constraint(values, Layout(major_to_minor=tuple(range(values.ndim))))


def select_rows(matrix, rows):
    return jnp.dot(matrix, rows, preferred_element_type=F32).astype(BF16)


def attend_kernel(
    scale, chosen, arrived, up_keys, up_values, keys, out, packed, query, peak, mass, total
):
    children = chosen.shape[0]
    heads, nope_width, latent_width = up_keys.shape
    kv_width = keys.shape[0]
    rope_width = kv_width - latent_width
    steps = query.shape[0] // (heads * children)
    tokens = steps * children
    rope_from = heads * steps * nope_width
    keys_from = rope_from + heads * steps * rope_width
    key_stride = (arrived.shape[1] - keys_from) // steps
    dims = (((1,), (1,)), ((), ()))

    @pl.when(pl.program_id(0) == 0)
    def _():
        packed[...] = jnp.dot(
            chosen[...], arrived[...], preferred_element_type=F32
        ).astype(BF16)
        for h in range(heads):
            for t in range(steps):
                rows = pl.ds(h * tokens + t * children, children)
                block = h * steps + t
                query[rows, latent_width:] = packed[
                    :, rope_from + block * rope_width : rope_from + (block + 1) * rope_width
                ]
            at = h * steps * nope_width
            nope = jnp.concatenate(
                [packed[:, at + t * nope_width : at + (t + 1) * nope_width] for t in range(steps)], axis=0
            )
            query[pl.ds(h * tokens, tokens), :latent_width] = jnp.dot(
                nope, up_keys[h], preferred_element_type=F32
            ).astype(BF16)
        own = jnp.concatenate(
            [
                packed[:, keys_from + u * key_stride : keys_from + u * key_stride + kv_width]
                for u in range(steps)
            ],
            axis=0,
        )
        scores = lax.dot_general(query[...], own, dims, preferred_element_type=F32) * scale
        row = lax.rem(lax.broadcasted_iota(jnp.int32, scores.shape, 0), tokens)
        column = lax.broadcasted_iota(jnp.int32, scores.shape, 1)
        seen = (lax.rem(row, children) == lax.rem(column, children)) & (
            lax.div(column, children) <= lax.div(row, children)
        )
        scores = jnp.where(seen, scores, -1e30)
        top = jnp.max(scores, axis=1, keepdims=True)
        weights = jnp.where(seen, jnp.exp(scores - top), 0.0)
        peak[...] = jnp.broadcast_to(top, peak.shape)
        mass[...] = jnp.broadcast_to(jnp.sum(weights, axis=1, keepdims=True), mass.shape)
        total[...] = jnp.dot(
            weights.astype(BF16), own[:, :latent_width], preferred_element_type=F32
        )

    half = query.shape[0] // 2
    for first in (0, half):
        rows = pl.ds(first, half)
        scores = jnp.dot(query[rows, :], keys[...], preferred_element_type=F32) * scale
        before = peak[rows, :1]
        top = jnp.maximum(before, jnp.max(scores, axis=1, keepdims=True))
        weights = jnp.exp(scores - top)
        shrink = jnp.exp(before - top)
        peak[rows, :] = jnp.broadcast_to(top, (half, peak.shape[1]))
        mass[rows, :] = mass[rows, :] * shrink + jnp.sum(weights, axis=1, keepdims=True)
        total[rows, :] = total[rows, :] * shrink + lax.dot_general(
            weights.astype(BF16), keys[:latent_width, :], dims, preferred_element_type=F32
        )

    @pl.when(pl.program_id(0) == pl.num_programs(0) - 1)
    def _():
        value_width = up_values.shape[2]
        for h in range(heads):
            rows = pl.ds(h * tokens, tokens)
            latent_out = (total[rows, :] / mass[rows, :1]).astype(BF16)
            out[:, h * value_width : (h + 1) * value_width] = jnp.dot(
                latent_out, up_values[h], preferred_element_type=F32
            ).astype(BF16)


def attend(chosen, arrived, prefix, up_keys, up_values, steps, scale):
    children = chosen.shape[0]
    heads, _, latent_width = up_keys.shape
    value_width = up_values.shape[2]
    kv_width, prefix_len = prefix.shape
    rows = heads * steps * children
    key_block = prefix_len // 4
    whole = lambda array: pl.BlockSpec(array.shape, lambda i: (0,) * array.ndim)
    return pl.pallas_call(
        functools.partial(attend_kernel, scale),
        grid=(prefix_len // key_block,),
        in_specs=[
            whole(chosen),
            whole(arrived),
            whole(up_keys),
            whole(up_values),
            pl.BlockSpec((kv_width, key_block), lambda i: (0, i)),
        ],
        out_specs=pl.BlockSpec((steps * children, heads * value_width), lambda i: (0, 0)),
        out_shape=jax.ShapeDtypeStruct((steps * children, heads * value_width), BF16),
        scratch_shapes=[
            pltpu.VMEM((children, arrived.shape[1]), BF16),
            pltpu.VMEM((rows, kv_width), BF16),
            pltpu.VMEM((rows, 128), F32),
            pltpu.VMEM((rows, 128), F32),
            pltpu.VMEM((rows, latent_width), F32),
        ],
        compiler_params=pltpu.CompilerParams(vmem_limit_bytes=40 * 2**20),
        cost_estimate=pl.CostEstimate(
            flops=2 * rows * prefix_len * (kv_width + latent_width),
            bytes_accessed=2 * prefix_len * kv_width + 4 * up_keys.size,
            transcendentals=rows * prefix_len,
        ),
    )(chosen, arrived, up_keys, up_values, prefix)


def ring_gather(values, axis):
    n = lax.axis_size(axis)
    blocks = [None] * n
    blocks[0] = ahead = back = values
    for step in range(1, n // 2 + 1):
        ahead = lax.ppermute(ahead, axis, [(i, (i + 1) % n) for i in range(n)])
        blocks[step] = ahead
        if step < n - step:
            back = lax.ppermute(back, axis, [(i, (i - 1) % n) for i in range(n)])
            blocks[n - step] = back
    return jnp.stack(blocks)


def local(
    queries,
    new_latents,
    parent_cache,
    parent_of,
    up_keys,
    up_values,
    out_proj,
    hidden_in,
    router,
    routes,
    w_gate,
    w_up,
    w_down,
):
    n_x, n_z, n_y, n_c = (lax.axis_size(a) for a in ("x", "z", "y", "c"))
    searchers = n_x * n_z
    children, steps, heads, query_width = queries.shape
    nope_width, latent_width = up_keys.shape[1:]
    rope_width = query_width - nope_width
    kv_width = parent_cache.shape[2]
    value_width = up_values.shape[2]
    tokens = children * steps
    width = hidden_in.shape[2]
    block = out_proj.shape[1]
    core = lax.axis_index("c")

    proj = lax.all_gather(out_proj, "x", axis=0, tiled=False)
    hidden_here = w_down.shape[1]
    here = lax.axis_index("y")
    gate_up = []
    for k in range(n_y):
        to = lax.rem(here + k, n_y)
        gate_k = lax.dynamic_slice_in_dim(w_gate[0], to * (D // n_y), D // n_y, axis=0)
        up_k = lax.dynamic_slice_in_dim(w_up[0], to * (D // n_y), D // n_y, axis=0)
        gate_up.append(along_y(row_major(jnp.concatenate([gate_k, up_k], axis=1)), k))

    def columns_of(step, for_core):
        start = (lax.rem(here + step, n_y) * n_c + for_core) * width
        return lax.dynamic_slice_in_dim(w_down[0], start, width, axis=1)

    down_swapped = to_other_core(
        row_major(jnp.concatenate([columns_of(k, 1 - core) for k in range(n_y)], axis=0))
    )

    placer = (jnp.arange(searchers, dtype=jnp.int32)[:, None] == parent_of[None, :]).astype(BF16)
    nope = queries[..., :nope_width].transpose(0, 2, 1, 3).reshape(children, -1)
    rope = queries[..., nope_width:].transpose(0, 2, 1, 3).reshape(children, -1)
    fill = jnp.ones((children, steps, -kv_width % 128), BF16)
    keys = jnp.concatenate([new_latents, fill], axis=2).reshape(children, -1)
    payload = select_rows(placer, jnp.concatenate([nope, rope, keys], axis=1))
    arrived = exchange(payload.reshape(searchers, 1, -1), SEARCH).reshape(searchers, -1)

    present = arrived[:, -1].astype(F32)
    span = jnp.arange(searchers, dtype=jnp.int32)
    before = jnp.sum(jnp.where(span[None, :] < span[:, None], present[None, :], 0.0), axis=1)
    chosen = (
        (jnp.arange(children, dtype=F32)[:, None] == before[None, :]) & (present[None, :] > 0)
    ).astype(BF16)
    homes = jnp.sum(chosen.astype(F32) * span.astype(F32)[None, :], axis=1)
    attention = attend(
        chosen,
        arrived,
        parent_cache[0].T,
        up_keys,
        up_values,
        steps,
        float(query_width) ** (-0.5),
    )

    home_rows = jnp.broadcast_to(jnp.tile(homes, steps)[:, None], (tokens, 128)).astype(BF16)
    attention = jnp.concatenate([attention, home_rows], axis=1)
    attention, down_swapped = lax.optimization_barrier((attention, down_swapped))
    gathered = ring_gather(attention, "z")
    gathered, gate_up, down_swapped, w_down = lax.optimization_barrier(
        (gathered, gate_up, down_swapped, w_down)
    )
    down = []
    hidden_here = w_down.shape[1]
    for k in range(n_y):
        start = (lax.rem(here + k, n_y) * n_c + core) * width
        own_k = lax.dynamic_slice_in_dim(w_down[0], start, width, axis=1)
        swapped_k = down_swapped[k * hidden_here : (k + 1) * hidden_here]
        down.append(along_y(row_major(jnp.concatenate([own_k, swapped_k], axis=0)), k))
    all_homes = gathered[:, :children, -1].astype(jnp.int32)
    gathered = gathered[:, :, : heads * value_width].reshape(n_z * tokens, -1)
    partial = jnp.einsum("rk,xkf->xrf", gathered, proj, preferred_element_type=F32).astype(BF16)

    rows_half = n_z * tokens // n_c
    pieces = exchange(partial.reshape(n_y * n_c, rows_half, block), MP)
    summed = jnp.sum(pieces.astype(F32), axis=0).astype(BF16)

    zs = n_z // n_c
    my_homes = lax.dynamic_slice_in_dim(all_homes, core * zs, zs, axis=0)
    scatter = (span[None, :, None] == my_homes[:, None, :]).astype(BF16)
    slots = jnp.einsum(
        "zsj,ztjf->sztf",
        scatter,
        summed.reshape(zs, steps, children, block),
        preferred_element_type=F32,
    ).astype(BF16)
    landed = exchange(slots.reshape(searchers, zs * steps, block), SEARCH)
    landed = landed.reshape(n_x, n_z, zs, steps, block).transpose(1, 0, 2, 3, 4)
    sender = jnp.arange(n_z, dtype=jnp.int32)[:, None, None, None]
    back = lax.rem(sender - lax.rem(parent_of, n_z)[None, :, None, None] + n_z, n_z)
    picker = (
        lax.div(parent_of, n_z)[None, :, None, None]
        == jnp.arange(n_x, dtype=jnp.int32)[None, None, :, None]
    ) & (back == core * zs + jnp.arange(zs, dtype=jnp.int32)[None, None, None, :])
    mine = jnp.einsum(
        "zis,zsf->zif",
        picker.reshape(n_z, children, -1).astype(BF16),
        landed.reshape(n_z, n_x * zs, -1),
        preferred_element_type=F32,
    ).astype(BF16)
    mine = mine.reshape(n_z, children, steps, block).transpose(1, 2, 0, 3).reshape(tokens, n_c, width)
    keep = jnp.where(core == 0, mine[:, 0], mine[:, 1])
    give = jnp.where(core == 0, mine[:, 1], mine[:, 0])
    projected = keep.astype(F32) + to_other_core(give).astype(F32)
    residual = (hidden_in.reshape(tokens, width).astype(F32) + projected).astype(BF16)
    residual, down = lax.optimization_barrier((residual, down))
    residual_wide = residual.astype(F32)

    experts = router.shape[1]
    topk = routes.shape[2]
    capacity = min(tokens, 3 * tokens * topk // (2 * experts))
    picked = routes.reshape(tokens, topk)
    named = jnp.any(
        picked[None, :, :] == jnp.arange(experts, dtype=jnp.int32)[:, None, None], axis=2
    )
    earlier = (
        jnp.arange(tokens, dtype=jnp.int32)[:, None] < jnp.arange(tokens, dtype=jnp.int32)[None, :]
    )
    rank = jnp.dot(named.astype(BF16), earlier.astype(BF16), preferred_element_type=F32)
    slot_of = (
        named[:, None, :]
        & (rank[:, None, :] == jnp.arange(capacity, dtype=F32)[None, :, None])
    ).reshape(experts * capacity, tokens)
    outgoing = select_rows(slot_of.astype(BF16), residual)
    quads = capacity // 4
    rows = exchange(outgoing.reshape(experts, quads, 4, width), SEARCH).reshape(
        experts * capacity, width
    )

    squares = jnp.sum(residual_wide * residual_wide, axis=1, keepdims=True)
    router_part = jnp.dot(residual, router, preferred_element_type=F32)
    stats = jnp.concatenate(
        [router_part, squares, jnp.zeros((tokens, 128 - experts - 1), F32)], axis=1
    )
    stats = stats + to_other_core(stats)
    stats = sum(along_y(stats, k) for k in range(n_y))
    home_rms = lax.rsqrt(stats[:, experts] / D + 1e-06)
    affinity = jax.nn.sigmoid(stats[:, :experts] * home_rms[:, None])
    chosen_affinity = jnp.where(named.T, affinity, 0.0)
    gate_weight = 2.5 * chosen_affinity / jnp.sum(chosen_affinity, axis=1, keepdims=True)

    rows, gate_weight = lax.optimization_barrier((rows, gate_weight))
    other = to_other_core(rows)
    low = jnp.where(core == 0, rows, other)
    high = jnp.where(core == 0, other, rows)
    both = jnp.concatenate([low, high], axis=1)
    both_wide = both.astype(F32)
    row_squares = jnp.sum(both_wide * both_wide, axis=1).reshape(-1, 128)
    squares_top = row_squares.astype(BF16)
    squares_rest = (row_squares - squares_top.astype(F32)).astype(BF16)
    ride = jnp.concatenate([squares_top, squares_rest], axis=1)
    lines = ride.shape[0]
    ride = jnp.pad(ride, ((0, -lines % 16), (0, 0)))
    slots_total = experts * capacity
    arrivals = []
    for k in range(1, n_y):
        act = jnp.dot(both, gate_up[k], preferred_element_type=F32).astype(BF16)
        arrivals.append(along_y(jnp.concatenate([act, ride], axis=0), n_y - k))
    arrivals = [arrival.astype(F32) for arrival in arrivals]
    acts = jnp.dot(both, gate_up[0], preferred_element_type=F32)
    for arrival in arrivals:
        acts = acts + arrival[:slots_total]
        row_squares = row_squares + (
            arrival[slots_total : slots_total + lines, :128]
            + arrival[slots_total : slots_total + lines, 128:]
        )
    row_rms = lax.rsqrt(row_squares.reshape(-1) / D + 1e-06)
    acts = acts * row_rms[:, None]
    hidden = (jax.nn.silu(acts[:, :hidden_here]) * acts[:, hidden_here:]).astype(BF16)
    hidden_core = jnp.concatenate([along_y(hidden, k) for k in range(n_y)], axis=1)
    hidden_other = to_other_core(hidden_core)
    down_here = jnp.concatenate([block_k[:hidden_here] for block_k in down], axis=0)
    down_there = jnp.concatenate([block_k[hidden_here:] for block_k in down], axis=0)
    expert_out = (
        jnp.dot(hidden_core, down_here, preferred_element_type=F32)
        + jnp.dot(hidden_other, down_there, preferred_element_type=F32)
    ).astype(BF16)
    returned = exchange(expert_out.reshape(experts, quads, 4, width), SEARCH).reshape(
        experts * capacity, width
    )

    weight_of = jnp.where(
        slot_of.reshape(experts, capacity, tokens), gate_weight.T[:, None, :], 0.0
    ).reshape(experts * capacity, tokens)
    upper = weight_of.astype(BF16)
    lower = (weight_of - upper.astype(F32)).astype(BF16)
    dims = (((0,), (0,)), ((), ()))
    expert_mix = lax.dot_general(
        upper, returned, dims, preferred_element_type=F32
    ) + lax.dot_general(lower, returned, dims, preferred_element_type=F32)
    mixed = (residual_wide + expert_mix).astype(BF16)
    return mixed.reshape(children, steps, width)


def solution(mesh):
    fine = Mesh(mesh.devices.reshape(4, 8, 4, 2), ("x", "z", "y", "c"))
    in_specs = (
        P(SEARCH, None, MP, None),
        P(SEARCH, None, None),
        P(SEARCH, None, None),
        P(SEARCH),
        P(MP, None, None),
        P(MP, None, None),
        P(MP, SEARCH),
        P(SEARCH, None, MP),
        P(MP, None),
        P(SEARCH, None, None),
        P(SEARCH, None, MP),
        P(SEARCH, None, MP),
        P(SEARCH, MP, None),
    )
    out_specs = P(SEARCH, None, MP)
    return jax.shard_map(local, mesh=fine, in_specs=in_specs, out_specs=out_specs, check_vma=False)
```

```python
import functools

import jax
import jax.numpy as jnp
from jax import lax
from jax.experimental import pallas as pl
from jax.experimental.layout import Layout, with_layout_constraint
from jax.experimental.pallas import tpu as pltpu
from jax.sharding import Mesh
from jax.sharding import PartitionSpec as P

D = 7168
SEARCH = ("x", "z")
MP = ("y", "c")
BF16 = jnp.bfloat16
F32 = jnp.float32


def exchange(values, axes):
    return lax.all_to_all(values, axes, split_axis=0, concat_axis=0, tiled=True)


def to_other_core(values):
    return lax.ppermute(values, "c", [(0, 1), (1, 0)])


def along_y(values, step):
    if step == 0:
        return values
    n = lax.axis_size("y")
    return lax.ppermute(values, "y", [(i, (i + step) % n) for i in range(n)])


def row_major(values):
    return with_layout_constraint(values, Layout(major_to_minor=tuple(range(values.ndim))))


def select_rows(matrix, rows):
    return jnp.dot(matrix, rows, preferred_element_type=F32).astype(BF16)


def attend_kernel(
    scale, chosen, arrived, up_keys, up_values, keys, out, packed, query, peak, mass, total
):
    children = chosen.shape[0]
    heads, nope_width, latent_width = up_keys.shape
    kv_width = keys.shape[0]
    rope_width = kv_width - latent_width
    steps = query.shape[0] // (heads * children)
    tokens = steps * children
    rope_from = heads * steps * nope_width
    keys_from = rope_from + heads * steps * rope_width
    key_stride = (arrived.shape[1] - keys_from) // steps
    dims = (((1,), (1,)), ((), ()))

    @pl.when(pl.program_id(0) == 0)
    def _():
        packed[...] = jnp.dot(
            chosen[...], arrived[...], preferred_element_type=F32
        ).astype(BF16)
        for h in range(heads):
            for t in range(steps):
                rows = pl.ds(h * tokens + t * children, children)
                block = h * steps + t
                query[rows, latent_width:] = packed[
                    :, rope_from + block * rope_width : rope_from + (block + 1) * rope_width
                ]
            at = h * steps * nope_width
            nope = jnp.concatenate(
                [packed[:, at + t * nope_width : at + (t + 1) * nope_width] for t in range(steps)], axis=0
            )
            query[pl.ds(h * tokens, tokens), :latent_width] = jnp.dot(
                nope, up_keys[h], preferred_element_type=F32
            ).astype(BF16)
        own = jnp.concatenate(
            [
                packed[:, keys_from + u * key_stride : keys_from + u * key_stride + kv_width]
                for u in range(steps)
            ],
            axis=0,
        )
        scores = lax.dot_general(query[...], own, dims, preferred_element_type=F32) * scale
        row = lax.rem(lax.broadcasted_iota(jnp.int32, scores.shape, 0), tokens)
        column = lax.broadcasted_iota(jnp.int32, scores.shape, 1)
        seen = (lax.rem(row, children) == lax.rem(column, children)) & (
            lax.div(column, children) <= lax.div(row, children)
        )
        scores = jnp.where(seen, scores, -1e30)
        top = jnp.max(scores, axis=1, keepdims=True)
        weights = jnp.where(seen, jnp.exp(scores - top), 0.0)
        peak[...] = jnp.broadcast_to(top, peak.shape)
        mass[...] = jnp.broadcast_to(jnp.sum(weights, axis=1, keepdims=True), mass.shape)
        total[...] = jnp.dot(
            weights.astype(BF16), own[:, :latent_width], preferred_element_type=F32
        )

    half = query.shape[0] // 2
    for first in (0, half):
        rows = pl.ds(first, half)
        scores = jnp.dot(query[rows, :], keys[...], preferred_element_type=F32) * scale
        before = peak[rows, :1]
        top = jnp.maximum(before, jnp.max(scores, axis=1, keepdims=True))
        weights = jnp.exp(scores - top)
        shrink = jnp.exp(before - top)
        peak[rows, :] = jnp.broadcast_to(top, (half, peak.shape[1]))
        mass[rows, :] = mass[rows, :] * shrink + jnp.sum(weights, axis=1, keepdims=True)
        total[rows, :] = total[rows, :] * shrink + lax.dot_general(
            weights.astype(BF16), keys[:latent_width, :], dims, preferred_element_type=F32
        )

    @pl.when(pl.program_id(0) == pl.num_programs(0) - 1)
    def _():
        value_width = up_values.shape[2]
        for h in range(heads):
            rows = pl.ds(h * tokens, tokens)
            latent_out = (total[rows, :] / mass[rows, :1]).astype(BF16)
            out[:, h * value_width : (h + 1) * value_width] = jnp.dot(
                latent_out, up_values[h], preferred_element_type=F32
            ).astype(BF16)


def attend(chosen, arrived, prefix, up_keys, up_values, steps, scale):
    children = chosen.shape[0]
    heads, _, latent_width = up_keys.shape
    value_width = up_values.shape[2]
    kv_width, prefix_len = prefix.shape
    rows = heads * steps * children
    key_block = prefix_len // 4
    whole = lambda array: pl.BlockSpec(array.shape, lambda i: (0,) * array.ndim)
    return pl.pallas_call(
        functools.partial(attend_kernel, scale),
        grid=(prefix_len // key_block,),
        in_specs=[
            whole(chosen),
            whole(arrived),
            whole(up_keys),
            whole(up_values),
            pl.BlockSpec((kv_width, key_block), lambda i: (0, i)),
        ],
        out_specs=pl.BlockSpec((steps * children, heads * value_width), lambda i: (0, 0)),
        out_shape=jax.ShapeDtypeStruct((steps * children, heads * value_width), BF16),
        scratch_shapes=[
            pltpu.VMEM((children, arrived.shape[1]), BF16),
            pltpu.VMEM((rows, kv_width), BF16),
            pltpu.VMEM((rows, 128), F32),
            pltpu.VMEM((rows, 128), F32),
            pltpu.VMEM((rows, latent_width), F32),
        ],
        compiler_params=pltpu.CompilerParams(vmem_limit_bytes=56 * 2**20),
        cost_estimate=pl.CostEstimate(
            flops=2 * rows * prefix_len * (kv_width + latent_width),
            bytes_accessed=2 * prefix_len * kv_width + 4 * up_keys.size,
            transcendentals=rows * prefix_len,
        ),
    )(chosen, arrived, up_keys, up_values, prefix)


def ring_gather(values, axis):
    n = lax.axis_size(axis)
    blocks = [None] * n
    blocks[0] = ahead = back = values
    for step in range(1, n // 2 + 1):
        ahead = lax.ppermute(ahead, axis, [(i, (i + 1) % n) for i in range(n)])
        blocks[step] = ahead
        if step < n - step:
            back = lax.ppermute(back, axis, [(i, (i - 1) % n) for i in range(n)])
            blocks[n - step] = back
    return blocks


def project_kernel(*refs):
    *blocks, proj, out = refs
    depth = proj.shape[2]
    halves = out.shape[0] // proj.shape[0]
    each = len(blocks) // halves
    for h in range(halves):
        rows = jnp.concatenate(
            [blocks[h * each + k][:, :depth] for k in range(each)], axis=0
        )
        for x in range(proj.shape[0]):
            out[x * halves + h] = lax.dot_general(
                proj[x], rows, (((1,), (1,)), ((), ())), preferred_element_type=F32
            ).astype(BF16)


def project(blocks, proj, halves):
    n_x, columns, depth = proj.shape
    rows = len(blocks) * blocks[0].shape[0] // halves
    return pl.pallas_call(
        project_kernel,
        out_shape=jax.ShapeDtypeStruct((n_x * halves, columns, rows), BF16),
        compiler_params=pltpu.CompilerParams(vmem_limit_bytes=12 * 2**20),
        cost_estimate=pl.CostEstimate(
            flops=2 * n_x * halves * columns * depth * rows,
            bytes_accessed=2 * proj.size + 2 * rows * halves * depth,
            transcendentals=0,
        ),
    )(*blocks, proj)


def activate_kernel(count, core, rows, other, *refs):
    weights, rest = refs[:count], refs[count:]
    ride, outs = (rest[0], rest[1:]) if len(rest) > count else (None, rest)
    width = rows.shape[1]
    mine = pl.ds(pl.multiple_of(core[0] * width, 128), width)
    theirs = pl.ds(pl.multiple_of((1 - core[0]) * width, 128), width)
    for w, out in zip(weights, outs):
        act = jnp.dot(rows[...], w[mine, :], preferred_element_type=F32) + jnp.dot(
            other[...], w[theirs, :], preferred_element_type=F32
        )
        out[: rows.shape[0], :] = act.astype(out.dtype)
        if ride is not None:
            out[rows.shape[0] :, :] = ride[...]


def activate(core, rows, other, weights, ride=None):
    count, columns = len(weights), weights[0].shape[1]
    vmem = pl.BlockSpec(memory_space=pltpu.VMEM)
    if ride is None:
        shape = jax.ShapeDtypeStruct((rows.shape[0], columns), F32)
        operands = (rows, other, *weights)
    else:
        shape = jax.ShapeDtypeStruct((rows.shape[0] + ride.shape[0], columns), BF16)
        operands = (rows, other, *weights, ride)
    return pl.pallas_call(
        functools.partial(activate_kernel, count),
        in_specs=[pl.BlockSpec(memory_space=pltpu.SMEM)] + [vmem] * len(operands),
        out_specs=[vmem] * count,
        out_shape=[shape] * count,
        compiler_params=pltpu.CompilerParams(vmem_limit_bytes=12 * 2**20),
        cost_estimate=pl.CostEstimate(
            flops=4 * count * rows.size * columns,
            bytes_accessed=4 * rows.size + 2 * count * weights[0].size,
            transcendentals=0,
        ),
    )(core.reshape(1), *operands)


def local(
    queries,
    new_latents,
    parent_cache,
    parent_of,
    up_keys,
    up_values,
    out_proj,
    hidden_in,
    router,
    routes,
    w_gate,
    w_up,
    w_down,
):
    n_x, n_z, n_y, n_c = (lax.axis_size(a) for a in ("x", "z", "y", "c"))
    searchers = n_x * n_z
    children, steps, heads, query_width = queries.shape
    nope_width, latent_width = up_keys.shape[1:]
    rope_width = query_width - nope_width
    kv_width = parent_cache.shape[2]
    value_width = up_values.shape[2]
    tokens = children * steps
    width = hidden_in.shape[2]
    block = out_proj.shape[1]
    core = lax.axis_index("c")

    proj = lax.all_gather(out_proj.T, "x", axis=0, tiled=False)
    hidden_here = w_down.shape[1]
    here = lax.axis_index("y")
    gate_up = []
    for k in range(n_y):
        to = lax.rem(here + k, n_y)
        gate_k = lax.dynamic_slice_in_dim(w_gate[0], to * (D // n_y), D // n_y, axis=0)
        up_k = lax.dynamic_slice_in_dim(w_up[0], to * (D // n_y), D // n_y, axis=0)
        gate_up.append(along_y(row_major(jnp.concatenate([gate_k, up_k], axis=1)), k))

    def columns_of(step, for_core):
        start = (lax.rem(here + step, n_y) * n_c + for_core) * width
        return lax.dynamic_slice_in_dim(w_down[0], start, width, axis=1)

    down_swapped = to_other_core(
        row_major(jnp.concatenate([columns_of(k, 1 - core) for k in range(n_y)], axis=0))
    )

    placer = (jnp.arange(searchers, dtype=jnp.int32)[:, None] == parent_of[None, :]).astype(BF16)
    nope = queries[..., :nope_width].transpose(0, 2, 1, 3).reshape(children, -1)
    rope = queries[..., nope_width:].transpose(0, 2, 1, 3).reshape(children, -1)
    fill = jnp.ones((children, steps, -kv_width % 128), BF16)
    keys = jnp.concatenate([new_latents, fill], axis=2).reshape(children, -1)
    payload = select_rows(placer, jnp.concatenate([nope, rope, keys], axis=1))
    arrived = exchange(payload.reshape(searchers, 2, -1), SEARCH).reshape(searchers, -1)

    present = arrived[:, -1].astype(F32)
    span = jnp.arange(searchers, dtype=jnp.int32)
    before = jnp.sum(jnp.where(span[None, :] < span[:, None], present[None, :], 0.0), axis=1)
    chosen = (
        (jnp.arange(children, dtype=F32)[:, None] == before[None, :]) & (present[None, :] > 0)
    ).astype(BF16)
    homes = jnp.sum(chosen.astype(F32) * span.astype(F32)[None, :], axis=1)
    attention = attend(
        chosen,
        arrived,
        parent_cache[0].T,
        up_keys,
        up_values,
        steps,
        float(query_width) ** (-0.5),
    )

    home_lanes = jnp.pad(jnp.tile(homes, steps), (0, -tokens % 128))
    home_rows = jnp.broadcast_to(home_lanes[None, :], (tokens, home_lanes.shape[0])).astype(BF16)
    attention = jnp.concatenate([attention, home_rows], axis=1)
    attention, down_swapped, routes, parent_of = lax.optimization_barrier(
        (attention, down_swapped, routes, parent_of)
    )
    gathered = ring_gather(attention, "z")
    partial = project(gathered, proj, n_c)
    partial, gate_up, down_swapped, w_down = lax.optimization_barrier(
        (partial, gate_up, down_swapped, w_down)
    )
    down = []
    hidden_here = w_down.shape[1]
    for k in range(n_y):
        start = (lax.rem(here + k, n_y) * n_c + core) * width
        own_k = lax.dynamic_slice_in_dim(w_down[0], start, width, axis=1)
        swapped_k = down_swapped[k * hidden_here : (k + 1) * hidden_here]
        down.append(along_y(row_major(jnp.concatenate([own_k, swapped_k], axis=0)), k))

    pieces = exchange(partial, MP)
    summed = jnp.sum(pieces.astype(F32), axis=0).astype(BF16)

    zs = n_z // n_c
    all_homes = jnp.stack([g[0, heads * value_width :][:tokens] for g in gathered])
    my_homes = lax.dynamic_slice_in_dim(all_homes, core * zs, zs, axis=0).reshape(-1)
    slot = jnp.arange(searchers * zs * steps, dtype=jnp.int32)
    row_at = jnp.arange(zs * tokens, dtype=jnp.int32)
    scatter = (
        my_homes.astype(jnp.int32)[None, :] == lax.div(slot, zs * steps)[:, None]
    ) & (lax.div(row_at, children)[None, :] == lax.rem(slot, zs * steps)[:, None])
    slots = lax.dot_general(
        scatter.astype(BF16), summed, (((1,), (1,)), ((), ())), preferred_element_type=F32
    ).astype(BF16)
    landed = exchange(slots.reshape(searchers, zs * steps, block), SEARCH)
    landed = landed.reshape(n_x, n_z, zs, steps, block).transpose(1, 0, 2, 3, 4)
    sender = jnp.arange(n_z, dtype=jnp.int32)[:, None, None, None]
    back = lax.rem(sender - lax.rem(parent_of, n_z)[None, :, None, None] + n_z, n_z)
    picker = (
        lax.div(parent_of, n_z)[None, :, None, None]
        == jnp.arange(n_x, dtype=jnp.int32)[None, None, :, None]
    ) & (back == core * zs + jnp.arange(zs, dtype=jnp.int32)[None, None, None, :])
    mine = jnp.einsum(
        "zis,zsf->zif",
        picker.reshape(n_z, children, -1).astype(BF16),
        landed.reshape(n_z, n_x * zs, -1),
        preferred_element_type=F32,
    ).astype(BF16)
    mine = mine.reshape(n_z, children, steps, block).transpose(1, 2, 0, 3).reshape(tokens, n_c, width)
    keep = jnp.where(core == 0, mine[:, 0], mine[:, 1])
    give = jnp.where(core == 0, mine[:, 1], mine[:, 0])
    projected = keep.astype(F32) + to_other_core(give).astype(F32)
    residual = (hidden_in.reshape(tokens, width).astype(F32) + projected).astype(BF16)
    residual_wide = residual.astype(F32)

    experts = router.shape[1]
    topk = routes.shape[2]
    capacity = min(tokens, 3 * tokens * topk // (2 * experts))
    picked = routes.reshape(tokens, topk)
    named = jnp.any(
        picked[None, :, :] == jnp.arange(experts, dtype=jnp.int32)[:, None, None], axis=2
    )
    earlier = (
        jnp.arange(tokens, dtype=jnp.int32)[:, None] < jnp.arange(tokens, dtype=jnp.int32)[None, :]
    )
    rank = jnp.dot(named.astype(BF16), earlier.astype(BF16), preferred_element_type=F32)
    slot_of = (
        named[:, None, :]
        & (rank[:, None, :] == jnp.arange(capacity, dtype=F32)[None, :, None])
    ).reshape(experts * capacity, tokens)
    outgoing = select_rows(slot_of.astype(BF16), residual)
    quads = capacity // 4
    rows = exchange(outgoing.reshape(experts, quads, 4, width), SEARCH).reshape(
        experts * capacity, width
    )

    squares = jnp.sum(residual_wide * residual_wide, axis=1, keepdims=True)
    router_part = jnp.dot(residual, router, preferred_element_type=F32)
    stats = jnp.concatenate(
        [router_part, squares, jnp.zeros((tokens, 128 - experts - 1), F32)], axis=1
    )
    stats = stats + to_other_core(stats)
    stats = sum(along_y(stats, k) for k in range(n_y))
    stats, down = lax.optimization_barrier((stats, down))
    home_rms = lax.rsqrt(stats[:, experts] / D + 1e-06)
    affinity = jax.nn.sigmoid(stats[:, :experts] * home_rms[:, None])
    chosen_affinity = jnp.where(named.T, affinity, 0.0)
    gate_weight = 2.5 * chosen_affinity / jnp.sum(chosen_affinity, axis=1, keepdims=True)

    rows, gate_weight = lax.optimization_barrier((rows, gate_weight))
    other = to_other_core(rows)
    own_squares = jnp.sum(jnp.square(rows.astype(F32)), axis=1)
    row_squares = (own_squares + jnp.sum(jnp.square(other.astype(F32)), axis=1)).reshape(-1, 128)
    squares_top = row_squares.astype(BF16)
    squares_rest = (row_squares - squares_top.astype(F32)).astype(BF16)
    ride = jnp.concatenate([squares_top, squares_rest], axis=1)
    lines = ride.shape[0]
    ride = jnp.pad(ride, ((0, -lines % 16), (0, 0)))
    slots_total = experts * capacity
    partials = activate(core, rows, other, gate_up[1:], ride)
    arrivals = [along_y(partials[k - 1], n_y - k) for k in range(1, n_y)]
    [acts] = activate(core, rows, other, gate_up[:1])
    for arrival in arrivals:
        acts = acts + arrival[:slots_total].astype(F32)
        squares = arrival[slots_total : slots_total + lines].astype(F32)
        row_squares = row_squares + squares[:, :128] + squares[:, 128:]
    row_rms = lax.rsqrt(row_squares.reshape(-1) / D + 1e-06)
    acts = acts * row_rms[:, None]
    hidden = (jax.nn.silu(acts[:, :hidden_here]) * acts[:, hidden_here:]).astype(BF16)
    hidden_core = jnp.concatenate([along_y(hidden, k) for k in range(n_y)], axis=1)
    hidden_other = to_other_core(hidden_core)
    down_here = jnp.concatenate([block_k[:hidden_here] for block_k in down], axis=0)
    down_there = jnp.concatenate([block_k[hidden_here:] for block_k in down], axis=0)
    expert_out = (
        jnp.dot(hidden_core, down_here, preferred_element_type=F32)
        + jnp.dot(hidden_other, down_there, preferred_element_type=F32)
    ).astype(BF16)
    returned = exchange(expert_out.reshape(experts, quads, 4, width), SEARCH).reshape(
        experts * capacity, width
    )

    weight_of = jnp.where(
        slot_of.reshape(experts, capacity, tokens), gate_weight.T[:, None, :], 0.0
    ).reshape(experts * capacity, tokens)
    upper = weight_of.astype(BF16)
    lower = (weight_of - upper.astype(F32)).astype(BF16)
    dims = (((0,), (0,)), ((), ()))
    expert_mix = lax.dot_general(
        upper, returned, dims, preferred_element_type=F32
    ) + lax.dot_general(lower, returned, dims, preferred_element_type=F32)
    mixed = (residual_wide + expert_mix).astype(BF16)
    return mixed.reshape(children, steps, width)


def solution(mesh):
    fine = Mesh(mesh.devices.reshape(4, 8, 4, 2), ("x", "z", "y", "c"))
    in_specs = (
        P(SEARCH, None, MP, None),
        P(SEARCH, None, None),
        P(SEARCH, None, None),
        P(SEARCH),
        P(MP, None, None),
        P(MP, None, None),
        P(MP, SEARCH),
        P(SEARCH, None, MP),
        P(MP, None),
        P(SEARCH, None, None),
        P(SEARCH, None, MP),
        P(SEARCH, None, MP),
        P(SEARCH, MP, None),
    )
    out_specs = P(SEARCH, None, MP)
    return jax.shard_map(local, mesh=fine, in_specs=in_specs, out_specs=out_specs, check_vma=False)
```

```python
import functools

import jax
import jax.numpy as jnp
from jax import lax
from jax.experimental import pallas as pl
from jax.experimental.layout import Layout, with_layout_constraint
from jax.experimental.pallas import tpu as pltpu
from jax.sharding import Mesh
from jax.sharding import PartitionSpec as P

D = 7168
SEARCH = ("x", "z")
MP = ("y", "c")
BF16 = jnp.bfloat16
F32 = jnp.float32


def exchange(values, axes):
    return lax.all_to_all(values, axes, split_axis=0, concat_axis=0, tiled=True)


def to_other_core(values):
    return lax.ppermute(values, "c", [(0, 1), (1, 0)])


def along_y(values, step):
    if step == 0:
        return values
    n = lax.axis_size("y")
    return lax.ppermute(values, "y", [(i, (i + step) % n) for i in range(n)])


def row_major(values):
    return with_layout_constraint(values, Layout(major_to_minor=tuple(range(values.ndim))))


def select_rows(matrix, rows):
    return jnp.dot(matrix, rows, preferred_element_type=F32).astype(BF16)


def attend_kernel(
    scale, chosen, arrived, up_keys, up_values, keys, out, packed, query, peak, mass, total
):
    children = chosen.shape[0]
    heads, nope_width, latent_width = up_keys.shape
    kv_width = keys.shape[0]
    rope_width = kv_width - latent_width
    steps = query.shape[0] // (heads * children)
    tokens = steps * children
    rope_from = heads * steps * nope_width
    keys_from = rope_from + heads * steps * rope_width
    key_stride = (arrived.shape[1] - keys_from) // steps
    dims = (((1,), (1,)), ((), ()))

    @pl.when(pl.program_id(0) == 0)
    def _():
        packed[...] = jnp.dot(
            chosen[...], arrived[...], preferred_element_type=F32
        ).astype(BF16)
        for h in range(heads):
            for t in range(steps):
                rows = pl.ds(h * tokens + t * children, children)
                block = h * steps + t
                query[rows, latent_width:] = packed[
                    :, rope_from + block * rope_width : rope_from + (block + 1) * rope_width
                ]
            at = h * steps * nope_width
            nope = jnp.concatenate(
                [packed[:, at + t * nope_width : at + (t + 1) * nope_width] for t in range(steps)], axis=0
            )
            query[pl.ds(h * tokens, tokens), :latent_width] = jnp.dot(
                nope, up_keys[h], preferred_element_type=F32
            ).astype(BF16)
        own = jnp.concatenate(
            [
                packed[:, keys_from + u * key_stride : keys_from + u * key_stride + kv_width]
                for u in range(steps)
            ],
            axis=0,
        )
        scores = lax.dot_general(query[...], own, dims, preferred_element_type=F32) * scale
        row = lax.rem(lax.broadcasted_iota(jnp.int32, scores.shape, 0), tokens)
        column = lax.broadcasted_iota(jnp.int32, scores.shape, 1)
        seen = (lax.rem(row, children) == lax.rem(column, children)) & (
            lax.div(column, children) <= lax.div(row, children)
        )
        scores = jnp.where(seen, scores, -1e30)
        top = jnp.max(scores, axis=1, keepdims=True)
        weights = jnp.where(seen, jnp.exp(scores - top), 0.0)
        peak[...] = jnp.broadcast_to(top, peak.shape)
        mass[...] = jnp.broadcast_to(jnp.sum(weights, axis=1, keepdims=True), mass.shape)
        total[...] = jnp.dot(
            weights.astype(BF16), own[:, :latent_width], preferred_element_type=F32
        )

    half = query.shape[0] // 2
    for first in (0, half):
        rows = pl.ds(first, half)
        scores = jnp.dot(query[rows, :], keys[...], preferred_element_type=F32) * scale
        before = peak[rows, :1]
        top = jnp.maximum(before, jnp.max(scores, axis=1, keepdims=True))
        weights = jnp.exp(scores - top)
        shrink = jnp.exp(before - top)
        peak[rows, :] = jnp.broadcast_to(top, (half, peak.shape[1]))
        mass[rows, :] = mass[rows, :] * shrink + jnp.sum(weights, axis=1, keepdims=True)
        total[rows, :] = total[rows, :] * shrink + lax.dot_general(
            weights.astype(BF16), keys[:latent_width, :], dims, preferred_element_type=F32
        )

    @pl.when(pl.program_id(0) == pl.num_programs(0) - 1)
    def _():
        value_width = up_values.shape[2]
        for h in range(heads):
            rows = pl.ds(h * tokens, tokens)
            latent_out = (total[rows, :] / mass[rows, :1]).astype(BF16)
            out[:, h * value_width : (h + 1) * value_width] = jnp.dot(
                latent_out, up_values[h], preferred_element_type=F32
            ).astype(BF16)


def attend(chosen, arrived, prefix, up_keys, up_values, steps, scale):
    children = chosen.shape[0]
    heads, _, latent_width = up_keys.shape
    value_width = up_values.shape[2]
    kv_width, prefix_len = prefix.shape
    rows = heads * steps * children
    key_block = prefix_len // 4
    whole = lambda array: pl.BlockSpec(array.shape, lambda i: (0,) * array.ndim)
    return pl.pallas_call(
        functools.partial(attend_kernel, scale),
        grid=(prefix_len // key_block,),
        in_specs=[
            whole(chosen),
            whole(arrived),
            whole(up_keys),
            whole(up_values),
            pl.BlockSpec((kv_width, key_block), lambda i: (0, i)),
        ],
        out_specs=pl.BlockSpec((steps * children, heads * value_width), lambda i: (0, 0)),
        out_shape=jax.ShapeDtypeStruct((steps * children, heads * value_width), BF16),
        scratch_shapes=[
            pltpu.VMEM((children, arrived.shape[1]), BF16),
            pltpu.VMEM((rows, kv_width), BF16),
            pltpu.VMEM((rows, 128), F32),
            pltpu.VMEM((rows, 128), F32),
            pltpu.VMEM((rows, latent_width), F32),
        ],
        compiler_params=pltpu.CompilerParams(vmem_limit_bytes=56 * 2**20),
        cost_estimate=pl.CostEstimate(
            flops=2 * rows * prefix_len * (kv_width + latent_width),
            bytes_accessed=2 * prefix_len * kv_width + 4 * up_keys.size,
            transcendentals=rows * prefix_len,
        ),
    )(chosen, arrived, up_keys, up_values, prefix)


def ring_gather(values, axis, due):
    n = lax.axis_size(axis)
    blocks = [None] * n
    blocks[0] = ahead = back = values
    for step in range(1, n // 2 + 1):
        ahead = lax.ppermute(ahead, axis, [(i, (i + 1) % n) for i in range(n)])
        if step == 2:
            ahead, due = lax.optimization_barrier((ahead, due))
        blocks[step] = ahead
        if step < n - step:
            back = lax.ppermute(back, axis, [(i, (i - 1) % n) for i in range(n)])
            blocks[n - step] = back
    return blocks, due


def project_kernel(where, *refs):
    *blocks, proj, keep, give, homes, rows = refs
    depth = proj.shape[2]
    each, per = keep.shape[2], blocks[0].shape[0]

    @pl.when(pl.program_id(0) == 0)
    def _():
        for k, block in enumerate(blocks):
            rows[k * per : (k + 1) * per, :] = block[:, :depth]
        top = jnp.concatenate([block[:16, depth:].astype(F32)[:1] for block in blocks], axis=0)
        half = len(blocks) // 2
        homes[...] = jnp.where(where[1] == 0, top[:half], top[half:])

    mine = rows[pl.ds(pl.multiple_of(where[1] * each, each), each), :]
    theirs = rows[pl.ds(pl.multiple_of((1 - where[1]) * each, each), each), :]
    dims = (((1,), (1,)), ((), ()))
    give[0] = lax.dot_general(proj[0], theirs, dims, preferred_element_type=F32).astype(BF16)
    keep[0] = lax.dot_general(proj[0], mine, dims, preferred_element_type=F32)


def project(where, blocks, proj):
    n_x, columns, depth = proj.shape
    rows = len(blocks) * blocks[0].shape[0]
    extra = blocks[0].shape[1] - depth
    out = (n_x, columns, rows // 2)
    step = pl.BlockSpec((1, columns, rows // 2), lambda k, where: (k, 0, 0))
    return pl.pallas_call(
        project_kernel,
        grid_spec=pltpu.PrefetchScalarGridSpec(
            num_scalar_prefetch=1,
            grid=(n_x,),
            in_specs=[pl.BlockSpec(block.shape, lambda k, where: (0, 0)) for block in blocks]
            + [
                pl.BlockSpec(
                    (1, columns, depth), lambda k, where: (lax.rem(where[0] + k, n_x), 0, 0)
                )
            ],
            out_specs=[
                step,
                step,
                pl.BlockSpec((len(blocks) // 2, extra), lambda k, where: (0, 0)),
            ],
            scratch_shapes=[pltpu.VMEM((rows, depth), BF16)],
        ),
        out_shape=[
            jax.ShapeDtypeStruct(out, F32),
            jax.ShapeDtypeStruct(out, BF16),
            jax.ShapeDtypeStruct((len(blocks) // 2, extra), F32),
        ],
        compiler_params=pltpu.CompilerParams(vmem_limit_bytes=56 * 2**20),
        cost_estimate=pl.CostEstimate(
            flops=2 * n_x * columns * depth * rows,
            bytes_accessed=2 * proj.size + 2 * rows * depth,
            transcendentals=0,
        ),
    )(where, *blocks, proj)


def land_kernel(core, picker, landed, keep, give):
    n_z = picker.shape[0]
    n_x = landed.shape[0] // n_z
    parts = []
    for z in range(n_z):
        rows = jnp.concatenate(
            [landed[x * n_z + z].astype(F32) for x in range(n_x)], axis=0
        ).astype(BF16)
        parts.append(jnp.dot(picker[z], rows, preferred_element_type=F32))
    low = jnp.concatenate(parts[: n_z // 2], axis=1)
    high = jnp.concatenate(parts[n_z // 2 :], axis=1)
    keep[...] = jnp.where(core[0] == 0, low, high)
    give[...] = jnp.where(core[0] == 0, high, low).astype(BF16)


def land(core, picker, landed):
    out = (picker.shape[1], picker.shape[0] // 2 * landed.shape[2])
    vmem = pl.BlockSpec(memory_space=pltpu.VMEM)
    return pl.pallas_call(
        land_kernel,
        in_specs=[pl.BlockSpec(memory_space=pltpu.SMEM), vmem, vmem],
        out_specs=[vmem] * 2,
        out_shape=[jax.ShapeDtypeStruct(out, F32), jax.ShapeDtypeStruct(out, BF16)],
        compiler_params=pltpu.CompilerParams(vmem_limit_bytes=8 * 2**20),
        cost_estimate=pl.CostEstimate(
            flops=2 * picker.size * landed.shape[2], bytes_accessed=4 * landed.size, transcendentals=0
        ),
    )(core.reshape(1), picker, landed)


def finish_kernel(own, other, *refs):
    *blocks, out = refs
    units = blocks[0].shape[0] // 2
    total = None
    for k, block in enumerate(blocks):
        span = slice(k * units, (k + 1) * units)
        part = jnp.dot(
            jnp.concatenate([own[:, span], other[:, span]], axis=1),
            block[...],
            preferred_element_type=F32,
        )
        total = part if total is None else total + part
    out[...] = total.astype(BF16)


def finish(own, other, blocks):
    vmem = pl.BlockSpec(memory_space=pltpu.VMEM)
    rows, columns = own.shape[0], blocks[0].shape[1]
    return pl.pallas_call(
        finish_kernel,
        in_specs=[vmem] * (2 + len(blocks)),
        out_specs=vmem,
        out_shape=jax.ShapeDtypeStruct((rows, columns), BF16),
        compiler_params=pltpu.CompilerParams(vmem_limit_bytes=14 * 2**20),
        cost_estimate=pl.CostEstimate(
            flops=4 * own.size * columns,
            bytes_accessed=4 * own.size + 2 * len(blocks) * blocks[0].size,
            transcendentals=0,
        ),
    )(own, other, *blocks)


def activate_kernel(count, core, rows, other, *refs):
    weights, rest = refs[:count], refs[count:]
    ride, outs = (rest[0], rest[1:]) if len(rest) > count else (None, rest)
    width = rows.shape[1]
    mine = pl.ds(pl.multiple_of(core[0] * width, 128), width)
    theirs = pl.ds(pl.multiple_of((1 - core[0]) * width, 128), width)
    for w, out in zip(weights, outs):
        act = jnp.dot(rows[...], w[mine, :], preferred_element_type=F32) + jnp.dot(
            other[...], w[theirs, :], preferred_element_type=F32
        )
        out[: rows.shape[0], :] = act.astype(out.dtype)
        if ride is not None:
            out[rows.shape[0] :, :] = ride[...]


def activate(core, rows, other, weights, ride=None):
    count, columns = len(weights), weights[0].shape[1]
    vmem = pl.BlockSpec(memory_space=pltpu.VMEM)
    if ride is None:
        shape = jax.ShapeDtypeStruct((rows.shape[0], columns), F32)
        operands = (rows, other, *weights)
    else:
        shape = jax.ShapeDtypeStruct((rows.shape[0] + ride.shape[0], columns), BF16)
        operands = (rows, other, *weights, ride)
    return pl.pallas_call(
        functools.partial(activate_kernel, count),
        in_specs=[pl.BlockSpec(memory_space=pltpu.SMEM)] + [vmem] * len(operands),
        out_specs=[vmem] * count,
        out_shape=[shape] * count,
        compiler_params=pltpu.CompilerParams(vmem_limit_bytes=12 * 2**20),
        cost_estimate=pl.CostEstimate(
            flops=4 * count * rows.size * columns,
            bytes_accessed=4 * rows.size + 2 * count * weights[0].size,
            transcendentals=0,
        ),
    )(core.reshape(1), *operands)


def local(
    queries,
    new_latents,
    parent_cache,
    parent_of,
    up_keys,
    up_values,
    out_proj,
    hidden_in,
    router,
    routes,
    w_gate,
    w_up,
    w_down,
):
    n_x, n_z, n_y, n_c = (lax.axis_size(a) for a in ("x", "z", "y", "c"))
    searchers = n_x * n_z
    children, steps, heads, query_width = queries.shape
    nope_width, latent_width = up_keys.shape[1:]
    rope_width = query_width - nope_width
    kv_width = parent_cache.shape[2]
    value_width = up_values.shape[2]
    tokens = children * steps
    width = hidden_in.shape[2]
    block = out_proj.shape[1]
    core = lax.axis_index("c")

    proj = lax.all_gather(out_proj.T, "x", axis=0, tiled=False)
    hidden_here = w_down.shape[1]
    here = lax.axis_index("y")
    gate_up = []
    for k in range(n_y):
        to = lax.rem(here + k, n_y)
        gate_k = lax.dynamic_slice_in_dim(w_gate[0], to * (D // n_y), D // n_y, axis=0)
        up_k = lax.dynamic_slice_in_dim(w_up[0], to * (D // n_y), D // n_y, axis=0)
        gate_up.append(along_y(row_major(jnp.concatenate([gate_k, up_k], axis=1)), k))

    def columns_of(step, for_core):
        start = (lax.rem(here + step, n_y) * n_c + for_core) * width
        return lax.dynamic_slice_in_dim(w_down[0], start, width, axis=1)

    down_swapped = to_other_core(
        row_major(jnp.concatenate([columns_of(k, 1 - core) for k in range(n_y)], axis=0))
    )

    placer = (jnp.arange(searchers, dtype=jnp.int32)[:, None] == parent_of[None, :]).astype(BF16)
    nope = queries[..., :nope_width].transpose(0, 2, 1, 3).reshape(children, -1)
    rope = queries[..., nope_width:].transpose(0, 2, 1, 3).reshape(children, -1)
    fill = jnp.ones((children, steps, -kv_width % 128), BF16)
    keys = jnp.concatenate([new_latents, fill], axis=2).reshape(children, -1)
    payload = select_rows(placer, jnp.concatenate([nope, rope, keys], axis=1))
    arrived = exchange(payload.reshape(searchers, 2, -1), SEARCH).reshape(searchers, -1)

    present = arrived[:, -1].astype(F32)
    span = jnp.arange(searchers, dtype=jnp.int32)
    before = jnp.sum(jnp.where(span[None, :] < span[:, None], present[None, :], 0.0), axis=1)
    chosen = (
        (jnp.arange(children, dtype=F32)[:, None] == before[None, :]) & (present[None, :] > 0)
    ).astype(BF16)
    homes = jnp.sum(chosen.astype(F32) * span.astype(F32)[None, :], axis=1)
    attention = attend(
        chosen,
        arrived,
        parent_cache[0].T,
        up_keys,
        up_values,
        steps,
        float(query_width) ** (-0.5),
    )

    home_lanes = jnp.pad(jnp.tile(homes, steps), (0, -tokens % 128))
    home_rows = jnp.broadcast_to(home_lanes[None, :], (tokens, home_lanes.shape[0])).astype(BF16)
    attention = jnp.concatenate([attention, home_rows], axis=1)
    attention, down_swapped, routes, parent_of = lax.optimization_barrier(
        (attention, down_swapped, routes, parent_of)
    )
    gathered, proj = ring_gather(attention, "z", proj)
    place = jnp.stack([here, core]).astype(jnp.int32)
    keep, give, my_homes = project(place, gathered, proj)
    hidden_here = w_down.shape[1]
    down = []
    for k in range(n_y):
        start = (lax.rem(here + k, n_y) * n_c + core) * width
        own_k = lax.dynamic_slice_in_dim(w_down[0], start, width, axis=1)
        swapped_k = down_swapped[k * hidden_here : (k + 1) * hidden_here]
        down.append(jnp.concatenate([own_k, swapped_k], axis=0))
    keep, give, gate_up, down = lax.optimization_barrier((keep, give, gate_up, down))

    paired = (keep + to_other_core(give).astype(F32)).astype(BF16)
    summed = sum(along_y(paired[k], k).astype(F32) for k in range(n_y)).astype(BF16)

    zs = n_z // n_c
    my_homes = my_homes[:, :tokens].reshape(-1)
    slot = jnp.arange(searchers * zs * steps, dtype=jnp.int32)
    row_at = jnp.arange(zs * tokens, dtype=jnp.int32)
    scatter = (
        my_homes.astype(jnp.int32)[None, :] == lax.div(slot, zs * steps)[:, None]
    ) & (lax.div(row_at, children)[None, :] == lax.rem(slot, zs * steps)[:, None])
    slots = lax.dot_general(
        scatter.astype(BF16), summed, (((1,), (1,)), ((), ())), preferred_element_type=F32
    ).astype(BF16)
    slots, down = lax.optimization_barrier((slots, down))
    down = [along_y(row_major(block_k), k) for k, block_k in enumerate(down)]
    landed = exchange(slots.reshape(searchers, zs * steps, block), SEARCH)
    landed, down[1], down[3] = lax.optimization_barrier((landed, down[1], down[3]))
    sender = jnp.arange(n_z, dtype=jnp.int32)[:, None, None]
    parent_row = jnp.repeat(parent_of, steps)[None, :, None]
    step_row = lax.rem(jnp.arange(tokens, dtype=jnp.int32), steps)[None, :, None]
    column = jnp.arange(n_x * zs * steps, dtype=jnp.int32)[None, None, :]
    back = lax.rem(sender - lax.rem(parent_row, n_z) + n_z, n_z)
    picker = (
        (lax.div(parent_row, n_z) == lax.div(column, zs * steps))
        & (back == core * zs + lax.rem(lax.div(column, steps), zs))
        & (step_row == lax.rem(column, steps))
    ).astype(BF16)
    keep, give = land(core, picker, landed)
    projected = keep + to_other_core(give).astype(F32)
    residual = (hidden_in.reshape(tokens, width).astype(F32) + projected).astype(BF16)
    residual_wide = residual.astype(F32)

    experts = router.shape[1]
    topk = routes.shape[2]
    capacity = min(tokens, 3 * tokens * topk // (2 * experts))
    picked = routes.reshape(tokens, topk)
    named = jnp.any(
        picked[None, :, :] == jnp.arange(experts, dtype=jnp.int32)[:, None, None], axis=2
    )
    earlier = (
        jnp.arange(tokens, dtype=jnp.int32)[:, None] < jnp.arange(tokens, dtype=jnp.int32)[None, :]
    )
    rank = jnp.dot(named.astype(BF16), earlier.astype(BF16), preferred_element_type=F32)
    slot_of = (
        named[:, None, :]
        & (rank[:, None, :] == jnp.arange(capacity, dtype=F32)[None, :, None])
    ).reshape(experts * capacity, tokens)
    outgoing = select_rows(slot_of.astype(BF16), residual)
    quads = capacity // 4
    rows = exchange(outgoing.reshape(experts, quads, 4, width), SEARCH).reshape(
        experts * capacity, width
    )

    squares = jnp.sum(residual_wide * residual_wide, axis=1, keepdims=True)
    router_part = jnp.dot(residual, router, preferred_element_type=F32)
    stats = jnp.concatenate(
        [router_part, squares, jnp.zeros((tokens, 128 - experts - 1), F32)], axis=1
    )
    stats = stats + to_other_core(stats)
    stats = sum(along_y(stats, k) for k in range(n_y))
    stats, down = lax.optimization_barrier((stats, down))
    home_rms = lax.rsqrt(stats[:, experts] / D + 1e-06)
    affinity = jax.nn.sigmoid(stats[:, :experts] * home_rms[:, None])
    chosen_affinity = jnp.where(named.T, affinity, 0.0)
    gate_weight = 2.5 * chosen_affinity / jnp.sum(chosen_affinity, axis=1, keepdims=True)

    rows, gate_weight = lax.optimization_barrier((rows, gate_weight))
    other = to_other_core(rows)
    own_squares = jnp.sum(jnp.square(rows.astype(F32)), axis=1)
    row_squares = (own_squares + jnp.sum(jnp.square(other.astype(F32)), axis=1)).reshape(-1, 128)
    squares_top = row_squares.astype(BF16)
    squares_rest = (row_squares - squares_top.astype(F32)).astype(BF16)
    ride = jnp.concatenate([squares_top, squares_rest], axis=1)
    lines = ride.shape[0]
    ride = jnp.pad(ride, ((0, -lines % 16), (0, 0)))
    slots_total = experts * capacity
    partials = activate(core, rows, other, gate_up[1:], ride)
    arrivals = [along_y(partials[k - 1], n_y - k) for k in range(1, n_y)]
    [acts] = activate(core, rows, other, gate_up[:1])
    for arrival in arrivals:
        acts = acts + arrival[:slots_total].astype(F32)
        squares = arrival[slots_total : slots_total + lines].astype(F32)
        row_squares = row_squares + squares[:, :128] + squares[:, 128:]
    row_rms = lax.rsqrt(row_squares.reshape(-1) / D + 1e-06)
    acts = acts * row_rms[:, None]
    hidden = (jax.nn.silu(acts[:, :hidden_here]) * acts[:, hidden_here:]).astype(BF16)
    hidden_core = jnp.concatenate([along_y(hidden, k) for k in range(n_y)], axis=1)
    hidden_other = to_other_core(hidden_core)
    expert_out = finish(hidden_core, hidden_other, down)
    returned = exchange(expert_out.reshape(experts, quads, 4, width), SEARCH).reshape(
        experts * capacity, width
    )

    weight_of = jnp.where(
        slot_of.reshape(experts, capacity, tokens), gate_weight.T[:, None, :], 0.0
    ).reshape(experts * capacity, tokens)
    upper = weight_of.astype(BF16)
    lower = (weight_of - upper.astype(F32)).astype(BF16)
    dims = (((0,), (0,)), ((), ()))
    expert_mix = lax.dot_general(
        upper, returned, dims, preferred_element_type=F32
    ) + lax.dot_general(lower, returned, dims, preferred_element_type=F32)
    mixed = (residual_wide + expert_mix).astype(BF16)
    return mixed.reshape(children, steps, width)


def solution(mesh):
    fine = Mesh(mesh.devices.reshape(4, 8, 4, 2), ("x", "z", "y", "c"))
    in_specs = (
        P(SEARCH, None, MP, None),
        P(SEARCH, None, None),
        P(SEARCH, None, None),
        P(SEARCH),
        P(MP, None, None),
        P(MP, None, None),
        P(MP, SEARCH),
        P(SEARCH, None, MP),
        P(MP, None),
        P(SEARCH, None, None),
        P(SEARCH, None, MP),
        P(SEARCH, None, MP),
        P(SEARCH, MP, None),
    )
    out_specs = P(SEARCH, None, MP)
    return jax.shard_map(local, mesh=fine, in_specs=in_specs, out_specs=out_specs, check_vma=False)
```

```python
import functools

import jax
import jax.numpy as jnp
from jax import lax
from jax.experimental import pallas as pl
from jax.experimental.layout import Layout, with_layout_constraint
from jax.experimental.pallas import tpu as pltpu
from jax.sharding import Mesh
from jax.sharding import PartitionSpec as P

D = 7168
SEARCH = ("x", "z")
MP = ("y", "c")
BF16 = jnp.bfloat16
F32 = jnp.float32


def exchange(values, axes):
    return lax.all_to_all(values, axes, split_axis=0, concat_axis=0, tiled=True)


def to_other_core(values):
    return lax.ppermute(values, "c", [(0, 1), (1, 0)])


def along_y(values, step):
    if step == 0:
        return values
    n = lax.axis_size("y")
    return lax.ppermute(values, "y", [(i, (i + step) % n) for i in range(n)])


def row_major(values):
    return with_layout_constraint(values, Layout(major_to_minor=tuple(range(values.ndim))))


def select_rows(matrix, rows):
    return jnp.dot(matrix, rows, preferred_element_type=F32).astype(BF16)


def attend_kernel(
    scale, chosen, arrived, up_keys, up_values, keys, out, packed, query, peak, mass, total
):
    children = chosen.shape[0]
    heads, nope_width, latent_width = up_keys.shape
    kv_width = keys.shape[0]
    rope_width = kv_width - latent_width
    steps = query.shape[0] // (heads * children)
    tokens = steps * children
    rope_from = heads * steps * nope_width
    keys_from = rope_from + heads * steps * rope_width
    key_stride = (arrived.shape[1] - keys_from) // steps
    dims = (((1,), (1,)), ((), ()))

    @pl.when(pl.program_id(0) == 0)
    def _():
        packed[...] = jnp.dot(
            chosen[...], arrived[...], preferred_element_type=F32
        ).astype(BF16)
        for h in range(heads):
            for t in range(steps):
                rows = pl.ds(h * tokens + t * children, children)
                block = h * steps + t
                query[rows, latent_width:] = packed[
                    :, rope_from + block * rope_width : rope_from + (block + 1) * rope_width
                ]
            at = h * steps * nope_width
            nope = jnp.concatenate(
                [packed[:, at + t * nope_width : at + (t + 1) * nope_width] for t in range(steps)], axis=0
            )
            query[pl.ds(h * tokens, tokens), :latent_width] = jnp.dot(
                nope, up_keys[h], preferred_element_type=F32
            ).astype(BF16)
        own = jnp.concatenate(
            [
                packed[:, keys_from + u * key_stride : keys_from + u * key_stride + kv_width]
                for u in range(steps)
            ],
            axis=0,
        )
        scores = lax.dot_general(query[...], own, dims, preferred_element_type=F32) * scale
        row = lax.rem(lax.broadcasted_iota(jnp.int32, scores.shape, 0), tokens)
        column = lax.broadcasted_iota(jnp.int32, scores.shape, 1)
        seen = (lax.rem(row, children) == lax.rem(column, children)) & (
            lax.div(column, children) <= lax.div(row, children)
        )
        scores = jnp.where(seen, scores, -1e30)
        top = jnp.max(scores, axis=1, keepdims=True)
        weights = jnp.where(seen, jnp.exp(scores - top), 0.0)
        peak[...] = jnp.broadcast_to(top, peak.shape)
        mass[...] = jnp.broadcast_to(jnp.sum(weights, axis=1, keepdims=True), mass.shape)
        total[...] = jnp.dot(
            weights.astype(BF16), own[:, :latent_width], preferred_element_type=F32
        )

    half = query.shape[0] // 2
    for first in (0, half):
        rows = pl.ds(first, half)
        scores = jnp.dot(query[rows, :], keys[...], preferred_element_type=F32) * scale
        before = peak[rows, :1]
        top = jnp.maximum(before, jnp.max(scores, axis=1, keepdims=True))
        weights = jnp.exp(scores - top)
        shrink = jnp.exp(before - top)
        peak[rows, :] = jnp.broadcast_to(top, (half, peak.shape[1]))
        mass[rows, :] = mass[rows, :] * shrink + jnp.sum(weights, axis=1, keepdims=True)
        total[rows, :] = total[rows, :] * shrink + lax.dot_general(
            weights.astype(BF16), keys[:latent_width, :], dims, preferred_element_type=F32
        )

    @pl.when(pl.program_id(0) == pl.num_programs(0) - 1)
    def _():
        value_width = up_values.shape[2]
        for h in range(heads):
            rows = pl.ds(h * tokens, tokens)
            latent_out = (total[rows, :] / mass[rows, :1]).astype(BF16)
            out[:, h * value_width : (h + 1) * value_width] = jnp.dot(
                latent_out, up_values[h], preferred_element_type=F32
            ).astype(BF16)


def attend(chosen, arrived, prefix, up_keys, up_values, steps, scale):
    children = chosen.shape[0]
    heads, _, latent_width = up_keys.shape
    value_width = up_values.shape[2]
    kv_width, prefix_len = prefix.shape
    rows = heads * steps * children
    key_block = prefix_len // 4
    whole = lambda array: pl.BlockSpec(array.shape, lambda i: (0,) * array.ndim)
    return pl.pallas_call(
        functools.partial(attend_kernel, scale),
        grid=(prefix_len // key_block,),
        in_specs=[
            whole(chosen),
            whole(arrived),
            whole(up_keys),
            whole(up_values),
            pl.BlockSpec((kv_width, key_block), lambda i: (0, i)),
        ],
        out_specs=pl.BlockSpec((steps * children, heads * value_width), lambda i: (0, 0)),
        out_shape=jax.ShapeDtypeStruct((steps * children, heads * value_width), BF16),
        scratch_shapes=[
            pltpu.VMEM((children, arrived.shape[1]), BF16),
            pltpu.VMEM((rows, kv_width), BF16),
            pltpu.VMEM((rows, 128), F32),
            pltpu.VMEM((rows, 128), F32),
            pltpu.VMEM((rows, latent_width), F32),
        ],
        compiler_params=pltpu.CompilerParams(vmem_limit_bytes=56 * 2**20),
        cost_estimate=pl.CostEstimate(
            flops=2 * rows * prefix_len * (kv_width + latent_width),
            bytes_accessed=2 * prefix_len * kv_width + 4 * up_keys.size,
            transcendentals=rows * prefix_len,
        ),
    )(chosen, arrived, up_keys, up_values, prefix)


def ring_gather(values, axis, due):
    n = lax.axis_size(axis)
    blocks = [None] * n
    blocks[0] = ahead = back = values
    for step in range(1, n // 2 + 1):
        ahead = lax.ppermute(ahead, axis, [(i, (i + 1) % n) for i in range(n)])
        if step == 2:
            ahead, due = lax.optimization_barrier((ahead, due))
        blocks[step] = ahead
        if step < n - step:
            back = lax.ppermute(back, axis, [(i, (i - 1) % n) for i in range(n)])
            blocks[n - step] = back
    return blocks, due


def cut_kernel(where, gate, up, down, *refs):
    *blocks, give, sems = refs
    n_y = len(blocks)
    rows, hidden = blocks[0].shape[0], gate.shape[2]
    units, width = down.shape[1], give.shape[1]
    copies = []
    for k, block in enumerate(blocks):
        to = lax.rem(where[0] + k, n_y)
        start = pl.multiple_of(to * rows, 128)
        column = pl.multiple_of((2 * to + 1 - where[1]) * width, 128)
        pieces = (
            (gate.at[0, pl.ds(start, rows), :], block.at[:, :hidden]),
            (up.at[0, pl.ds(start, rows), :], block.at[:, hidden:]),
            (down.at[0, :, pl.ds(column, width)], give.at[k * units : (k + 1) * units, :]),
        )
        for piece in pieces:
            copies.append(pltpu.make_async_copy(*piece, sems.at[len(copies)]))
            copies[-1].start()
    for copy in copies:
        copy.wait()


def cut(where, gate, up, down, n_y, width):
    away = pl.BlockSpec(memory_space=pl.ANY)
    block = jax.ShapeDtypeStruct((gate.shape[1] // n_y, 2 * gate.shape[2]), gate.dtype)
    give = jax.ShapeDtypeStruct((n_y * down.shape[1], width), down.dtype)
    *blocks, give = pl.pallas_call(
        cut_kernel,
        in_specs=[pl.BlockSpec(memory_space=pltpu.SMEM)] + [away] * 3,
        out_specs=[away] * (n_y + 1),
        out_shape=[block] * n_y + [give],
        scratch_shapes=[pltpu.SemaphoreType.DMA((3 * n_y,))],
        compiler_params=pltpu.CompilerParams(vmem_limit_bytes=56 * 2**20),
        cost_estimate=pl.CostEstimate(
            flops=0, bytes_accessed=4 * (gate.size + up.size) + 2 * down.size, transcendentals=0
        ),
    )(where, gate, up, down)
    return blocks, give


def project_kernel(where, *refs):
    *blocks, proj, keep, give, homes, rows = refs
    depth = proj.shape[2]
    each, per = keep.shape[2], blocks[0].shape[0]

    @pl.when(pl.program_id(0) == 0)
    def _():
        for k, block in enumerate(blocks):
            rows[k * per : (k + 1) * per, :] = block[:, :depth]
        top = jnp.concatenate([block[:16, depth:].astype(F32)[:1] for block in blocks], axis=0)
        half = len(blocks) // 2
        homes[...] = jnp.where(where[1] == 0, top[:half], top[half:])

    mine = rows[pl.ds(pl.multiple_of(where[1] * each, each), each), :]
    theirs = rows[pl.ds(pl.multiple_of((1 - where[1]) * each, each), each), :]
    dims = (((1,), (1,)), ((), ()))
    give[0] = lax.dot_general(proj[0], theirs, dims, preferred_element_type=F32).astype(BF16)
    keep[0] = lax.dot_general(proj[0], mine, dims, preferred_element_type=F32)


def project(where, blocks, proj):
    n_x, columns, depth = proj.shape
    rows = len(blocks) * blocks[0].shape[0]
    extra = blocks[0].shape[1] - depth
    out = (n_x, columns, rows // 2)
    step = pl.BlockSpec((1, columns, rows // 2), lambda k, where: (k, 0, 0))
    return pl.pallas_call(
        project_kernel,
        grid_spec=pltpu.PrefetchScalarGridSpec(
            num_scalar_prefetch=1,
            grid=(n_x,),
            in_specs=[pl.BlockSpec(block.shape, lambda k, where: (0, 0)) for block in blocks]
            + [
                pl.BlockSpec(
                    (1, columns, depth), lambda k, where: (lax.rem(where[0] + k, n_x), 0, 0)
                )
            ],
            out_specs=[
                step,
                step,
                pl.BlockSpec((len(blocks) // 2, extra), lambda k, where: (0, 0)),
            ],
            scratch_shapes=[pltpu.VMEM((rows, depth), BF16)],
        ),
        out_shape=[
            jax.ShapeDtypeStruct(out, F32),
            jax.ShapeDtypeStruct(out, BF16),
            jax.ShapeDtypeStruct((len(blocks) // 2, extra), F32),
        ],
        compiler_params=pltpu.CompilerParams(vmem_limit_bytes=56 * 2**20),
        cost_estimate=pl.CostEstimate(
            flops=2 * n_x * columns * depth * rows,
            bytes_accessed=2 * proj.size + 2 * rows * depth,
            transcendentals=0,
        ),
    )(where, *blocks, proj)


def land_kernel(core, picker, landed, keep, give):
    n_z = picker.shape[0]
    n_x = landed.shape[0] // n_z
    parts = []
    for z in range(n_z):
        rows = jnp.concatenate(
            [landed[x * n_z + z].astype(F32) for x in range(n_x)], axis=0
        ).astype(BF16)
        parts.append(jnp.dot(picker[z], rows, preferred_element_type=F32))
    low = jnp.concatenate(parts[: n_z // 2], axis=1)
    high = jnp.concatenate(parts[n_z // 2 :], axis=1)
    keep[...] = jnp.where(core[0] == 0, low, high)
    give[...] = jnp.where(core[0] == 0, high, low).astype(BF16)


def land(core, picker, landed):
    out = (picker.shape[1], picker.shape[0] // 2 * landed.shape[2])
    vmem = pl.BlockSpec(memory_space=pltpu.VMEM)
    return pl.pallas_call(
        land_kernel,
        in_specs=[pl.BlockSpec(memory_space=pltpu.SMEM), vmem, vmem],
        out_specs=[vmem] * 2,
        out_shape=[jax.ShapeDtypeStruct(out, F32), jax.ShapeDtypeStruct(out, BF16)],
        compiler_params=pltpu.CompilerParams(vmem_limit_bytes=8 * 2**20),
        cost_estimate=pl.CostEstimate(
            flops=2 * picker.size * landed.shape[2], bytes_accessed=4 * landed.size, transcendentals=0
        ),
    )(core.reshape(1), picker, landed)


def finish_kernel(own, other, *refs):
    *blocks, out = refs
    units = blocks[0].shape[0] // 2
    total = None
    for k, block in enumerate(blocks):
        span = slice(k * units, (k + 1) * units)
        part = jnp.dot(
            jnp.concatenate([own[:, span], other[:, span]], axis=1),
            block[...],
            preferred_element_type=F32,
        )
        total = part if total is None else total + part
    out[...] = total.astype(BF16)


def finish(own, other, blocks):
    vmem = pl.BlockSpec(memory_space=pltpu.VMEM)
    rows, columns = own.shape[0], blocks[0].shape[1]
    return pl.pallas_call(
        finish_kernel,
        in_specs=[vmem] * (2 + len(blocks)),
        out_specs=vmem,
        out_shape=jax.ShapeDtypeStruct((rows, columns), BF16),
        compiler_params=pltpu.CompilerParams(vmem_limit_bytes=14 * 2**20),
        cost_estimate=pl.CostEstimate(
            flops=4 * own.size * columns,
            bytes_accessed=4 * own.size + 2 * len(blocks) * blocks[0].size,
            transcendentals=0,
        ),
    )(own, other, *blocks)


def activate_kernel(count, core, rows, other, *refs):
    weights, rest = refs[:count], refs[count:]
    ride, outs = (rest[0], rest[1:]) if len(rest) > count else (None, rest)
    width = rows.shape[1]
    mine = pl.ds(pl.multiple_of(core[0] * width, 128), width)
    theirs = pl.ds(pl.multiple_of((1 - core[0]) * width, 128), width)
    for w, out in zip(weights, outs):
        act = jnp.dot(rows[...], w[mine, :], preferred_element_type=F32) + jnp.dot(
            other[...], w[theirs, :], preferred_element_type=F32
        )
        out[: rows.shape[0], :] = act.astype(out.dtype)
        if ride is not None:
            out[rows.shape[0] :, :] = ride[...]


def activate(core, rows, other, weights, ride=None):
    count, columns = len(weights), weights[0].shape[1]
    vmem = pl.BlockSpec(memory_space=pltpu.VMEM)
    if ride is None:
        shape = jax.ShapeDtypeStruct((rows.shape[0], columns), F32)
        operands = (rows, other, *weights)
    else:
        shape = jax.ShapeDtypeStruct((rows.shape[0] + ride.shape[0], columns), BF16)
        operands = (rows, other, *weights, ride)
    return pl.pallas_call(
        functools.partial(activate_kernel, count),
        in_specs=[pl.BlockSpec(memory_space=pltpu.SMEM)] + [vmem] * len(operands),
        out_specs=[vmem] * count,
        out_shape=[shape] * count,
        compiler_params=pltpu.CompilerParams(vmem_limit_bytes=12 * 2**20),
        cost_estimate=pl.CostEstimate(
            flops=4 * count * rows.size * columns,
            bytes_accessed=4 * rows.size + 2 * count * weights[0].size,
            transcendentals=0,
        ),
    )(core.reshape(1), *operands)


def local(
    queries,
    new_latents,
    parent_cache,
    parent_of,
    up_keys,
    up_values,
    out_proj,
    hidden_in,
    router,
    routes,
    w_gate,
    w_up,
    w_down,
):
    n_x, n_z, n_y, n_c = (lax.axis_size(a) for a in ("x", "z", "y", "c"))
    searchers = n_x * n_z
    children, steps, heads, query_width = queries.shape
    nope_width, latent_width = up_keys.shape[1:]
    rope_width = query_width - nope_width
    kv_width = parent_cache.shape[2]
    value_width = up_values.shape[2]
    tokens = children * steps
    width = hidden_in.shape[2]
    block = out_proj.shape[1]
    core = lax.axis_index("c")

    proj = lax.all_gather(out_proj.T, "x", axis=0, tiled=False)
    hidden_here = w_down.shape[1]
    here = lax.axis_index("y")
    place = jnp.stack([here, core]).astype(jnp.int32)
    gate_up, down_give = cut(place, w_gate, w_up, w_down, n_y, width)
    gate_up = [along_y(block_k, k) for k, block_k in enumerate(gate_up)]
    down_swapped = to_other_core(down_give)

    placer = (jnp.arange(searchers, dtype=jnp.int32)[:, None] == parent_of[None, :]).astype(BF16)
    nope = queries[..., :nope_width].transpose(0, 2, 1, 3).reshape(children, -1)
    rope = queries[..., nope_width:].transpose(0, 2, 1, 3).reshape(children, -1)
    fill = jnp.ones((children, steps, -kv_width % 128), BF16)
    keys = jnp.concatenate([new_latents, fill], axis=2).reshape(children, -1)
    payload = select_rows(placer, jnp.concatenate([nope, rope, keys], axis=1))
    arrived = exchange(payload.reshape(searchers, 2, -1), SEARCH).reshape(searchers, -1)

    present = arrived[:, -1].astype(F32)
    span = jnp.arange(searchers, dtype=jnp.int32)
    before = jnp.sum(jnp.where(span[None, :] < span[:, None], present[None, :], 0.0), axis=1)
    chosen = (
        (jnp.arange(children, dtype=F32)[:, None] == before[None, :]) & (present[None, :] > 0)
    ).astype(BF16)
    homes = jnp.sum(chosen.astype(F32) * span.astype(F32)[None, :], axis=1)
    attention = attend(
        chosen,
        arrived,
        parent_cache[0].T,
        up_keys,
        up_values,
        steps,
        float(query_width) ** (-0.5),
    )

    home_lanes = jnp.pad(jnp.tile(homes, steps), (0, -tokens % 128))
    home_rows = jnp.broadcast_to(home_lanes[None, :], (tokens, home_lanes.shape[0])).astype(BF16)
    attention = jnp.concatenate([attention, home_rows], axis=1)
    attention, down_swapped, routes, parent_of = lax.optimization_barrier(
        (attention, down_swapped, routes, parent_of)
    )
    gathered, proj = ring_gather(attention, "z", proj)
    keep, give, my_homes = project(place, gathered, proj)
    hidden_here = w_down.shape[1]
    down = []
    for k in range(n_y):
        start = (lax.rem(here + k, n_y) * n_c + core) * width
        own_k = lax.dynamic_slice_in_dim(w_down[0], start, width, axis=1)
        swapped_k = down_swapped[k * hidden_here : (k + 1) * hidden_here]
        down.append(jnp.concatenate([own_k, swapped_k], axis=0))
    experts = router.shape[1]
    topk = routes.shape[2]
    capacity = min(tokens, 3 * tokens * topk // (2 * experts))
    picked = routes.reshape(tokens, topk)
    named = jnp.any(
        picked[None, :, :] == jnp.arange(experts, dtype=jnp.int32)[:, None, None], axis=2
    )
    earlier = (
        jnp.arange(tokens, dtype=jnp.int32)[:, None] < jnp.arange(tokens, dtype=jnp.int32)[None, :]
    )
    rank = jnp.dot(named.astype(BF16), earlier.astype(BF16), preferred_element_type=F32)
    slot_of = (
        named[:, None, :]
        & (rank[:, None, :] == jnp.arange(capacity, dtype=F32)[None, :, None])
    ).reshape(experts * capacity, tokens)
    dispatcher = slot_of.astype(BF16)

    keep, give, gate_up, down, dispatcher = lax.optimization_barrier(
        (keep, give, gate_up, down, dispatcher)
    )

    paired = (keep + to_other_core(give).astype(F32)).astype(BF16)
    summed = sum(along_y(paired[k], k).astype(F32) for k in range(n_y)).astype(BF16)

    zs = n_z // n_c
    my_homes = my_homes[:, :tokens].reshape(-1)
    slot = jnp.arange(searchers * zs * steps, dtype=jnp.int32)
    row_at = jnp.arange(zs * tokens, dtype=jnp.int32)
    scatter = (
        my_homes.astype(jnp.int32)[None, :] == lax.div(slot, zs * steps)[:, None]
    ) & (lax.div(row_at, children)[None, :] == lax.rem(slot, zs * steps)[:, None])
    slots = lax.dot_general(
        scatter.astype(BF16), summed, (((1,), (1,)), ((), ())), preferred_element_type=F32
    ).astype(BF16)
    slots, down = lax.optimization_barrier((slots, down))
    down = [along_y(row_major(block_k), k) for k, block_k in enumerate(down)]
    landed = exchange(slots.reshape(searchers, zs * steps, block), SEARCH)
    sender = jnp.arange(n_z, dtype=jnp.int32)[:, None, None]
    parent_row = jnp.repeat(parent_of, steps)[None, :, None]
    step_row = lax.rem(jnp.arange(tokens, dtype=jnp.int32), steps)[None, :, None]
    column = jnp.arange(n_x * zs * steps, dtype=jnp.int32)[None, None, :]
    back = lax.rem(sender - lax.rem(parent_row, n_z) + n_z, n_z)
    picker = (
        (lax.div(parent_row, n_z) == lax.div(column, zs * steps))
        & (back == core * zs + lax.rem(lax.div(column, steps), zs))
        & (step_row == lax.rem(column, steps))
    ).astype(BF16)
    keep, give = land(core, picker, landed)
    projected = keep + to_other_core(give).astype(F32)
    residual = (hidden_in.reshape(tokens, width).astype(F32) + projected).astype(BF16)
    residual, down[1], down[3] = lax.optimization_barrier((residual, down[1], down[3]))
    residual_wide = residual.astype(F32)

    outgoing = select_rows(dispatcher, residual)
    quads = capacity // 4
    rows = exchange(outgoing.reshape(experts, quads, 4, width), SEARCH).reshape(
        experts * capacity, width
    )

    squares = jnp.sum(residual_wide * residual_wide, axis=1, keepdims=True)
    router_part = jnp.dot(residual, router, preferred_element_type=F32)
    stats = jnp.concatenate(
        [router_part, squares, jnp.zeros((tokens, 128 - experts - 1), F32)], axis=1
    )
    stats = stats + to_other_core(stats)
    stats = sum(along_y(stats, k) for k in range(n_y))
    stats, down = lax.optimization_barrier((stats, down))
    home_rms = lax.rsqrt(stats[:, experts] / D + 1e-06)
    affinity = jax.nn.sigmoid(stats[:, :experts] * home_rms[:, None])
    chosen_affinity = jnp.where(named.T, affinity, 0.0)
    gate_weight = 2.5 * chosen_affinity / jnp.sum(chosen_affinity, axis=1, keepdims=True)

    rows, gate_weight = lax.optimization_barrier((rows, gate_weight))
    other = to_other_core(rows)
    own_squares = jnp.sum(jnp.square(rows.astype(F32)), axis=1)
    row_squares = (own_squares + jnp.sum(jnp.square(other.astype(F32)), axis=1)).reshape(-1, 128)
    squares_top = row_squares.astype(BF16)
    squares_rest = (row_squares - squares_top.astype(F32)).astype(BF16)
    ride = jnp.concatenate([squares_top, squares_rest], axis=1)
    lines = ride.shape[0]
    ride = jnp.pad(ride, ((0, -lines % 16), (0, 0)))
    slots_total = experts * capacity
    partials = activate(core, rows, other, gate_up[1:], ride)
    arrivals = [along_y(partials[k - 1], n_y - k) for k in range(1, n_y)]
    [acts] = activate(core, rows, other, gate_up[:1])
    for arrival in arrivals:
        acts = acts + arrival[:slots_total].astype(F32)
        squares = arrival[slots_total : slots_total + lines].astype(F32)
        row_squares = row_squares + squares[:, :128] + squares[:, 128:]
    row_rms = lax.rsqrt(row_squares.reshape(-1) / D + 1e-06)
    acts = acts * row_rms[:, None]
    hidden = (jax.nn.silu(acts[:, :hidden_here]) * acts[:, hidden_here:]).astype(BF16)
    hidden_core = jnp.concatenate([along_y(hidden, k) for k in range(n_y)], axis=1)
    hidden_other = to_other_core(hidden_core)
    expert_out = finish(hidden_core, hidden_other, down)
    returned = exchange(expert_out.reshape(experts, quads, 4, width), SEARCH).reshape(
        experts * capacity, width
    )

    weight_of = jnp.where(
        slot_of.reshape(experts, capacity, tokens), gate_weight.T[:, None, :], 0.0
    ).reshape(experts * capacity, tokens)
    upper = weight_of.astype(BF16)
    lower = (weight_of - upper.astype(F32)).astype(BF16)
    dims = (((0,), (0,)), ((), ()))
    expert_mix = lax.dot_general(
        upper, returned, dims, preferred_element_type=F32
    ) + lax.dot_general(lower, returned, dims, preferred_element_type=F32)
    mixed = (residual_wide + expert_mix).astype(BF16)
    return mixed.reshape(children, steps, width)


def solution(mesh):
    fine = Mesh(mesh.devices.reshape(4, 8, 4, 2), ("x", "z", "y", "c"))
    in_specs = (
        P(SEARCH, None, MP, None),
        P(SEARCH, None, None),
        P(SEARCH, None, None),
        P(SEARCH),
        P(MP, None, None),
        P(MP, None, None),
        P(MP, SEARCH),
        P(SEARCH, None, MP),
        P(MP, None),
        P(SEARCH, None, None),
        P(SEARCH, None, MP),
        P(SEARCH, None, MP),
        P(SEARCH, MP, None),
    )
    out_specs = P(SEARCH, None, MP)
    return jax.shard_map(local, mesh=fine, in_specs=in_specs, out_specs=out_specs, check_vma=False)
```

```python
import functools

import jax
import jax.numpy as jnp
from jax import lax
from jax.experimental import pallas as pl
from jax.experimental.layout import Layout, with_layout_constraint
from jax.experimental.pallas import tpu as pltpu
from jax.sharding import Mesh
from jax.sharding import PartitionSpec as P

D = 7168
SEARCH = ("x", "z")
MP = ("y", "c")
BF16 = jnp.bfloat16
F32 = jnp.float32


def exchange(values, axes):
    return lax.all_to_all(values, axes, split_axis=0, concat_axis=0, tiled=True)


def to_other_core(values):
    return lax.ppermute(values, "c", [(0, 1), (1, 0)])


def along_y(values, step):
    if step == 0:
        return values
    n = lax.axis_size("y")
    return lax.ppermute(values, "y", [(i, (i + step) % n) for i in range(n)])


def row_major(values):
    return with_layout_constraint(values, Layout(major_to_minor=tuple(range(values.ndim))))


def select_rows(matrix, rows):
    return jnp.dot(matrix, rows, preferred_element_type=F32).astype(BF16)


def attend_kernel(
    scale, chosen, arrived, up_keys, up_values, keys, out, packed, query, peak, mass, total
):
    children = chosen.shape[0]
    heads, nope_width, latent_width = up_keys.shape
    kv_width = keys.shape[0]
    rope_width = kv_width - latent_width
    steps = query.shape[0] // (heads * children)
    tokens = steps * children
    rope_from = heads * steps * nope_width
    keys_from = rope_from + heads * steps * rope_width
    key_stride = (arrived.shape[1] - keys_from) // steps
    dims = (((1,), (1,)), ((), ()))

    @pl.when(pl.program_id(0) == 0)
    def _():
        packed[...] = jnp.dot(
            chosen[...], arrived[...], preferred_element_type=F32
        ).astype(BF16)
        for h in range(heads):
            for t in range(steps):
                rows = pl.ds(h * tokens + t * children, children)
                block = h * steps + t
                query[rows, latent_width:] = packed[
                    :, rope_from + block * rope_width : rope_from + (block + 1) * rope_width
                ]
            at = h * steps * nope_width
            nope = jnp.concatenate(
                [packed[:, at + t * nope_width : at + (t + 1) * nope_width] for t in range(steps)], axis=0
            )
            query[pl.ds(h * tokens, tokens), :latent_width] = jnp.dot(
                nope, up_keys[h], preferred_element_type=F32
            ).astype(BF16)
        own = jnp.concatenate(
            [
                packed[:, keys_from + u * key_stride : keys_from + u * key_stride + kv_width]
                for u in range(steps)
            ],
            axis=0,
        )
        scores = lax.dot_general(query[...], own, dims, preferred_element_type=F32) * scale
        row = lax.rem(lax.broadcasted_iota(jnp.int32, scores.shape, 0), tokens)
        column = lax.broadcasted_iota(jnp.int32, scores.shape, 1)
        seen = (lax.rem(row, children) == lax.rem(column, children)) & (
            lax.div(column, children) <= lax.div(row, children)
        )
        scores = jnp.where(seen, scores, -1e30)
        top = jnp.max(scores, axis=1, keepdims=True)
        weights = jnp.where(seen, jnp.exp(scores - top), 0.0)
        peak[...] = jnp.broadcast_to(top, peak.shape)
        mass[...] = jnp.broadcast_to(jnp.sum(weights, axis=1, keepdims=True), mass.shape)
        total[...] = jnp.dot(
            weights.astype(BF16), own[:, :latent_width], preferred_element_type=F32
        )

    half = query.shape[0] // 2
    for first in (0, half):
        rows = pl.ds(first, half)
        scores = jnp.dot(query[rows, :], keys[...], preferred_element_type=F32) * scale
        before = peak[rows, :1]
        top = jnp.maximum(before, jnp.max(scores, axis=1, keepdims=True))
        weights = jnp.exp(scores - top)
        shrink = jnp.exp(before - top)
        peak[rows, :] = jnp.broadcast_to(top, (half, peak.shape[1]))
        mass[rows, :] = mass[rows, :] * shrink + jnp.sum(weights, axis=1, keepdims=True)
        total[rows, :] = total[rows, :] * shrink + lax.dot_general(
            weights.astype(BF16), keys[:latent_width, :], dims, preferred_element_type=F32
        )

    @pl.when(pl.program_id(0) == pl.num_programs(0) - 1)
    def _():
        value_width = up_values.shape[2]
        for h in range(heads):
            rows = pl.ds(h * tokens, tokens)
            latent_out = (total[rows, :] / mass[rows, :1]).astype(BF16)
            out[:, h * value_width : (h + 1) * value_width] = jnp.dot(
                latent_out, up_values[h], preferred_element_type=F32
            ).astype(BF16)


def attend(chosen, arrived, prefix, up_keys, up_values, steps, scale):
    children = chosen.shape[0]
    heads, _, latent_width = up_keys.shape
    value_width = up_values.shape[2]
    kv_width, prefix_len = prefix.shape
    rows = heads * steps * children
    key_block = prefix_len // 4
    whole = lambda array: pl.BlockSpec(array.shape, lambda i: (0,) * array.ndim)
    return pl.pallas_call(
        functools.partial(attend_kernel, scale),
        grid=(prefix_len // key_block,),
        in_specs=[
            whole(chosen),
            whole(arrived),
            whole(up_keys),
            whole(up_values),
            pl.BlockSpec((kv_width, key_block), lambda i: (0, i)),
        ],
        out_specs=pl.BlockSpec((steps * children, heads * value_width), lambda i: (0, 0)),
        out_shape=jax.ShapeDtypeStruct((steps * children, heads * value_width), BF16),
        scratch_shapes=[
            pltpu.VMEM((children, arrived.shape[1]), BF16),
            pltpu.VMEM((rows, kv_width), BF16),
            pltpu.VMEM((rows, 128), F32),
            pltpu.VMEM((rows, 128), F32),
            pltpu.VMEM((rows, latent_width), F32),
        ],
        compiler_params=pltpu.CompilerParams(vmem_limit_bytes=56 * 2**20),
        cost_estimate=pl.CostEstimate(
            flops=2 * rows * prefix_len * (kv_width + latent_width),
            bytes_accessed=2 * prefix_len * kv_width + 4 * up_keys.size,
            transcendentals=rows * prefix_len,
        ),
    )(chosen, arrived, up_keys, up_values, prefix)


def ring_gather(values, axis, due):
    n = lax.axis_size(axis)
    blocks = [None] * n
    blocks[0] = ahead = back = values
    for step in range(1, n // 2 + 1):
        ahead = lax.ppermute(ahead, axis, [(i, (i + 1) % n) for i in range(n)])
        if step == 2:
            ahead, due = lax.optimization_barrier((ahead, due))
        blocks[step] = ahead
        if step < n - step:
            back = lax.ppermute(back, axis, [(i, (i - 1) % n) for i in range(n)])
            blocks[n - step] = back
    return blocks, due


def cut_kernel(where, gate, up, down, *refs):
    *blocks, give, sems = refs
    n_y = len(blocks)
    rows, hidden = blocks[0].shape[0], gate.shape[2]
    units, width = down.shape[1], give.shape[1]
    copies = []
    for k, block in enumerate(blocks):
        to = lax.rem(where[0] + k, n_y)
        start = pl.multiple_of(to * rows, 128)
        column = pl.multiple_of((2 * to + 1 - where[1]) * width, 128)
        pieces = (
            (gate.at[0, pl.ds(start, rows), :], block.at[:, :hidden]),
            (up.at[0, pl.ds(start, rows), :], block.at[:, hidden:]),
            (down.at[0, :, pl.ds(column, width)], give.at[k * units : (k + 1) * units, :]),
        )
        for piece in pieces:
            copies.append(pltpu.make_async_copy(*piece, sems.at[len(copies)]))
            copies[-1].start()
    for copy in copies:
        copy.wait()


def cut(where, gate, up, down, n_y, width):
    away = pl.BlockSpec(memory_space=pl.ANY)
    block = jax.ShapeDtypeStruct((gate.shape[1] // n_y, 2 * gate.shape[2]), gate.dtype)
    give = jax.ShapeDtypeStruct((n_y * down.shape[1], width), down.dtype)
    *blocks, give = pl.pallas_call(
        cut_kernel,
        in_specs=[pl.BlockSpec(memory_space=pltpu.SMEM)] + [away] * 3,
        out_specs=[pl.BlockSpec(memory_space=pltpu.VMEM)] * (n_y + 1),
        out_shape=[block] * n_y + [give],
        scratch_shapes=[pltpu.SemaphoreType.DMA((3 * n_y,))],
        compiler_params=pltpu.CompilerParams(vmem_limit_bytes=56 * 2**20),
        cost_estimate=pl.CostEstimate(
            flops=0, bytes_accessed=4 * (gate.size + up.size) + 2 * down.size, transcendentals=0
        ),
    )(where, gate, up, down)
    return blocks, give


def project_kernel(where, *refs):
    *blocks, proj, keep, give, homes, rows = refs
    depth = proj.shape[2]
    each, per = keep.shape[2], blocks[0].shape[0]

    @pl.when(pl.program_id(0) == 0)
    def _():
        for k, block in enumerate(blocks):
            rows[k * per : (k + 1) * per, :] = block[:, :depth]
        top = jnp.concatenate([block[:16, depth:].astype(F32)[:1] for block in blocks], axis=0)
        half = len(blocks) // 2
        homes[...] = jnp.where(where[1] == 0, top[:half], top[half:])

    mine = rows[pl.ds(pl.multiple_of(where[1] * each, each), each), :]
    theirs = rows[pl.ds(pl.multiple_of((1 - where[1]) * each, each), each), :]
    dims = (((1,), (1,)), ((), ()))
    give[0] = lax.dot_general(proj[0], theirs, dims, preferred_element_type=F32).astype(BF16)
    keep[0] = lax.dot_general(proj[0], mine, dims, preferred_element_type=F32)


def project(where, blocks, proj):
    n_x, columns, depth = proj.shape
    rows = len(blocks) * blocks[0].shape[0]
    extra = blocks[0].shape[1] - depth
    out = (n_x, columns, rows // 2)
    step = pl.BlockSpec((1, columns, rows // 2), lambda k, where: (k, 0, 0))
    return pl.pallas_call(
        project_kernel,
        grid_spec=pltpu.PrefetchScalarGridSpec(
            num_scalar_prefetch=1,
            grid=(n_x,),
            in_specs=[pl.BlockSpec(block.shape, lambda k, where: (0, 0)) for block in blocks]
            + [
                pl.BlockSpec(
                    (1, columns, depth), lambda k, where: (lax.rem(where[0] + k, n_x), 0, 0)
                )
            ],
            out_specs=[
                step,
                step,
                pl.BlockSpec((len(blocks) // 2, extra), lambda k, where: (0, 0)),
            ],
            scratch_shapes=[pltpu.VMEM((rows, depth), BF16)],
        ),
        out_shape=[
            jax.ShapeDtypeStruct(out, F32),
            jax.ShapeDtypeStruct(out, BF16),
            jax.ShapeDtypeStruct((len(blocks) // 2, extra), F32),
        ],
        compiler_params=pltpu.CompilerParams(vmem_limit_bytes=56 * 2**20),
        cost_estimate=pl.CostEstimate(
            flops=2 * n_x * columns * depth * rows,
            bytes_accessed=2 * proj.size + 2 * rows * depth,
            transcendentals=0,
        ),
    )(where, *blocks, proj)


def land_kernel(core, picker, landed, keep, give):
    n_z = picker.shape[0]
    n_x = landed.shape[0] // n_z
    parts = []
    for z in range(n_z):
        rows = jnp.concatenate(
            [landed[x * n_z + z].astype(F32) for x in range(n_x)], axis=0
        ).astype(BF16)
        parts.append(jnp.dot(picker[z], rows, preferred_element_type=F32))
    low = jnp.concatenate(parts[: n_z // 2], axis=1)
    high = jnp.concatenate(parts[n_z // 2 :], axis=1)
    keep[...] = jnp.where(core[0] == 0, low, high)
    give[...] = jnp.where(core[0] == 0, high, low).astype(BF16)


def land(core, picker, landed):
    out = (picker.shape[1], picker.shape[0] // 2 * landed.shape[2])
    vmem = pl.BlockSpec(memory_space=pltpu.VMEM)
    return pl.pallas_call(
        land_kernel,
        in_specs=[pl.BlockSpec(memory_space=pltpu.SMEM), vmem, vmem],
        out_specs=[vmem] * 2,
        out_shape=[jax.ShapeDtypeStruct(out, F32), jax.ShapeDtypeStruct(out, BF16)],
        compiler_params=pltpu.CompilerParams(vmem_limit_bytes=8 * 2**20),
        cost_estimate=pl.CostEstimate(
            flops=2 * picker.size * landed.shape[2], bytes_accessed=4 * landed.size, transcendentals=0
        ),
    )(core.reshape(1), picker, landed)


def finish_kernel(own, other, *refs):
    *blocks, out = refs
    units = blocks[0].shape[0] // 2
    total = None
    for k, block in enumerate(blocks):
        span = slice(k * units, (k + 1) * units)
        part = jnp.dot(
            jnp.concatenate([own[:, span], other[:, span]], axis=1),
            block[...],
            preferred_element_type=F32,
        )
        total = part if total is None else total + part
    out[...] = total.astype(BF16)


def finish(own, other, blocks):
    vmem = pl.BlockSpec(memory_space=pltpu.VMEM)
    rows, columns = own.shape[0], blocks[0].shape[1]
    return pl.pallas_call(
        finish_kernel,
        in_specs=[vmem] * (2 + len(blocks)),
        out_specs=vmem,
        out_shape=jax.ShapeDtypeStruct((rows, columns), BF16),
        compiler_params=pltpu.CompilerParams(vmem_limit_bytes=14 * 2**20),
        cost_estimate=pl.CostEstimate(
            flops=4 * own.size * columns,
            bytes_accessed=4 * own.size + 2 * len(blocks) * blocks[0].size,
            transcendentals=0,
        ),
    )(own, other, *blocks)


def activate_kernel(count, core, rows, other, *refs):
    weights, rest = refs[:count], refs[count:]
    ride, outs = (rest[0], rest[1:]) if len(rest) > count else (None, rest)
    width = rows.shape[1]
    mine = pl.ds(pl.multiple_of(core[0] * width, 128), width)
    theirs = pl.ds(pl.multiple_of((1 - core[0]) * width, 128), width)
    for w, out in zip(weights, outs):
        act = jnp.dot(rows[...], w[mine, :], preferred_element_type=F32) + jnp.dot(
            other[...], w[theirs, :], preferred_element_type=F32
        )
        out[: rows.shape[0], :] = act.astype(out.dtype)
        if ride is not None:
            out[rows.shape[0] :, :] = ride[...]


def activate(core, rows, other, weights, ride=None):
    count, columns = len(weights), weights[0].shape[1]
    vmem = pl.BlockSpec(memory_space=pltpu.VMEM)
    if ride is None:
        shape = jax.ShapeDtypeStruct((rows.shape[0], columns), F32)
        operands = (rows, other, *weights)
    else:
        shape = jax.ShapeDtypeStruct((rows.shape[0] + ride.shape[0], columns), BF16)
        operands = (rows, other, *weights, ride)
    return pl.pallas_call(
        functools.partial(activate_kernel, count),
        in_specs=[pl.BlockSpec(memory_space=pltpu.SMEM)] + [vmem] * len(operands),
        out_specs=[vmem] * count,
        out_shape=[shape] * count,
        compiler_params=pltpu.CompilerParams(vmem_limit_bytes=12 * 2**20),
        cost_estimate=pl.CostEstimate(
            flops=4 * count * rows.size * columns,
            bytes_accessed=4 * rows.size + 2 * count * weights[0].size,
            transcendentals=0,
        ),
    )(core.reshape(1), *operands)


def local(
    queries,
    new_latents,
    parent_cache,
    parent_of,
    up_keys,
    up_values,
    out_proj,
    hidden_in,
    router,
    routes,
    w_gate,
    w_up,
    w_down,
):
    n_x, n_z, n_y, n_c = (lax.axis_size(a) for a in ("x", "z", "y", "c"))
    searchers = n_x * n_z
    children, steps, heads, query_width = queries.shape
    nope_width, latent_width = up_keys.shape[1:]
    rope_width = query_width - nope_width
    kv_width = parent_cache.shape[2]
    value_width = up_values.shape[2]
    tokens = children * steps
    width = hidden_in.shape[2]
    block = out_proj.shape[1]
    core = lax.axis_index("c")

    proj = lax.all_gather(out_proj.T, "x", axis=0, tiled=False)
    hidden_here = w_down.shape[1]
    here = lax.axis_index("y")
    place = jnp.stack([here, core]).astype(jnp.int32)
    gate_up, down_give = cut(place, w_gate, w_up, w_down, n_y, width)
    gate_up = [along_y(block_k, k) for k, block_k in enumerate(gate_up)]
    down_swapped = to_other_core(down_give)

    placer = (jnp.arange(searchers, dtype=jnp.int32)[:, None] == parent_of[None, :]).astype(BF16)
    nope = queries[..., :nope_width].transpose(0, 2, 1, 3).reshape(children, -1)
    rope = queries[..., nope_width:].transpose(0, 2, 1, 3).reshape(children, -1)
    fill = jnp.ones((children, steps, -kv_width % 128), BF16)
    keys = jnp.concatenate([new_latents, fill], axis=2).reshape(children, -1)
    payload = select_rows(placer, jnp.concatenate([nope, rope, keys], axis=1))
    arrived = exchange(payload.reshape(searchers, 2, -1), SEARCH).reshape(searchers, -1)

    present = arrived[:, -1].astype(F32)
    span = jnp.arange(searchers, dtype=jnp.int32)
    before = jnp.sum(jnp.where(span[None, :] < span[:, None], present[None, :], 0.0), axis=1)
    chosen = (
        (jnp.arange(children, dtype=F32)[:, None] == before[None, :]) & (present[None, :] > 0)
    ).astype(BF16)
    homes = jnp.sum(chosen.astype(F32) * span.astype(F32)[None, :], axis=1)
    attention = attend(
        chosen,
        arrived,
        parent_cache[0].T,
        up_keys,
        up_values,
        steps,
        float(query_width) ** (-0.5),
    )

    home_lanes = jnp.pad(jnp.tile(homes, steps), (0, -tokens % 128))
    home_rows = jnp.broadcast_to(home_lanes[None, :], (tokens, home_lanes.shape[0])).astype(BF16)
    attention = jnp.concatenate([attention, home_rows], axis=1)
    attention, down_swapped, routes, parent_of = lax.optimization_barrier(
        (attention, down_swapped, routes, parent_of)
    )
    gathered, proj = ring_gather(attention, "z", proj)
    keep, give, my_homes = project(place, gathered, proj)
    hidden_here = w_down.shape[1]
    down = []
    for k in range(n_y):
        start = (lax.rem(here + k, n_y) * n_c + core) * width
        own_k = lax.dynamic_slice_in_dim(w_down[0], start, width, axis=1)
        swapped_k = down_swapped[k * hidden_here : (k + 1) * hidden_here]
        down.append(jnp.concatenate([own_k, swapped_k], axis=0))
    experts = router.shape[1]
    topk = routes.shape[2]
    capacity = min(tokens, 3 * tokens * topk // (2 * experts))
    picked = routes.reshape(tokens, topk)
    named = jnp.any(
        picked[None, :, :] == jnp.arange(experts, dtype=jnp.int32)[:, None, None], axis=2
    )
    earlier = (
        jnp.arange(tokens, dtype=jnp.int32)[:, None] < jnp.arange(tokens, dtype=jnp.int32)[None, :]
    )
    rank = jnp.dot(named.astype(BF16), earlier.astype(BF16), preferred_element_type=F32)
    slot_of = (
        named[:, None, :]
        & (rank[:, None, :] == jnp.arange(capacity, dtype=F32)[None, :, None])
    ).reshape(experts * capacity, tokens)
    dispatcher = slot_of.astype(BF16)

    keep, give, gate_up, down, dispatcher = lax.optimization_barrier(
        (keep, give, gate_up, down, dispatcher)
    )

    paired = (keep + to_other_core(give).astype(F32)).astype(BF16)
    summed = sum(along_y(paired[k], k).astype(F32) for k in range(n_y)).astype(BF16)

    zs = n_z // n_c
    my_homes = my_homes[:, :tokens].reshape(-1)
    slot = jnp.arange(searchers * zs * steps, dtype=jnp.int32)
    row_at = jnp.arange(zs * tokens, dtype=jnp.int32)
    scatter = (
        my_homes.astype(jnp.int32)[None, :] == lax.div(slot, zs * steps)[:, None]
    ) & (lax.div(row_at, children)[None, :] == lax.rem(slot, zs * steps)[:, None])
    slots = lax.dot_general(
        scatter.astype(BF16), summed, (((1,), (1,)), ((), ())), preferred_element_type=F32
    ).astype(BF16)
    slots, down = lax.optimization_barrier((slots, down))
    down = [along_y(row_major(block_k), k) for k, block_k in enumerate(down)]
    landed = exchange(slots.reshape(searchers, zs * steps, block), SEARCH)
    sender = jnp.arange(n_z, dtype=jnp.int32)[:, None, None]
    parent_row = jnp.repeat(parent_of, steps)[None, :, None]
    step_row = lax.rem(jnp.arange(tokens, dtype=jnp.int32), steps)[None, :, None]
    column = jnp.arange(n_x * zs * steps, dtype=jnp.int32)[None, None, :]
    back = lax.rem(sender - lax.rem(parent_row, n_z) + n_z, n_z)
    picker = (
        (lax.div(parent_row, n_z) == lax.div(column, zs * steps))
        & (back == core * zs + lax.rem(lax.div(column, steps), zs))
        & (step_row == lax.rem(column, steps))
    ).astype(BF16)
    keep, give = land(core, picker, landed)
    projected = keep + to_other_core(give).astype(F32)
    residual = (hidden_in.reshape(tokens, width).astype(F32) + projected).astype(BF16)
    residual, down[1], down[3] = lax.optimization_barrier((residual, down[1], down[3]))
    residual_wide = residual.astype(F32)

    outgoing = select_rows(dispatcher, residual)
    quads = capacity // 4
    rows = exchange(outgoing.reshape(experts, quads, 4, width), SEARCH).reshape(
        experts * capacity, width
    )

    squares = jnp.sum(residual_wide * residual_wide, axis=1, keepdims=True)
    router_part = jnp.dot(residual, router, preferred_element_type=F32)
    stats = jnp.concatenate(
        [router_part, squares, jnp.zeros((tokens, 128 - experts - 1), F32)], axis=1
    )
    stats = stats + to_other_core(stats)
    stats = sum(along_y(stats, k) for k in range(n_y))
    stats, down = lax.optimization_barrier((stats, down))
    home_rms = lax.rsqrt(stats[:, experts] / D + 1e-06)
    affinity = jax.nn.sigmoid(stats[:, :experts] * home_rms[:, None])
    chosen_affinity = jnp.where(named.T, affinity, 0.0)
    gate_weight = 2.5 * chosen_affinity / jnp.sum(chosen_affinity, axis=1, keepdims=True)

    rows, gate_weight = lax.optimization_barrier((rows, gate_weight))
    other = to_other_core(rows)
    own_squares = jnp.sum(jnp.square(rows.astype(F32)), axis=1)
    row_squares = (own_squares + jnp.sum(jnp.square(other.astype(F32)), axis=1)).reshape(-1, 128)
    squares_top = row_squares.astype(BF16)
    squares_rest = (row_squares - squares_top.astype(F32)).astype(BF16)
    ride = jnp.concatenate([squares_top, squares_rest], axis=1)
    lines = ride.shape[0]
    ride = jnp.pad(ride, ((0, -lines % 16), (0, 0)))
    slots_total = experts * capacity
    partials = activate(core, rows, other, gate_up[1:], ride)
    arrivals = [along_y(partials[k - 1], n_y - k) for k in range(1, n_y)]
    [acts] = activate(core, rows, other, gate_up[:1])
    for arrival in arrivals:
        acts = acts + arrival[:slots_total].astype(F32)
        squares = arrival[slots_total : slots_total + lines].astype(F32)
        row_squares = row_squares + squares[:, :128] + squares[:, 128:]
    row_rms = lax.rsqrt(row_squares.reshape(-1) / D + 1e-06)
    acts = acts * row_rms[:, None]
    hidden = (jax.nn.silu(acts[:, :hidden_here]) * acts[:, hidden_here:]).astype(BF16)
    hidden_core = jnp.concatenate([along_y(hidden, k) for k in range(n_y)], axis=1)
    hidden_other = to_other_core(hidden_core)
    expert_out = finish(hidden_core, hidden_other, down)
    returned = exchange(expert_out.reshape(experts, quads, 4, width), SEARCH).reshape(
        experts * capacity, width
    )

    weight_of = jnp.where(
        slot_of.reshape(experts, capacity, tokens), gate_weight.T[:, None, :], 0.0
    ).reshape(experts * capacity, tokens)
    upper = weight_of.astype(BF16)
    lower = (weight_of - upper.astype(F32)).astype(BF16)
    dims = (((0,), (0,)), ((), ()))
    expert_mix = lax.dot_general(
        upper, returned, dims, preferred_element_type=F32
    ) + lax.dot_general(lower, returned, dims, preferred_element_type=F32)
    mixed = (residual_wide + expert_mix).astype(BF16)
    return mixed.reshape(children, steps, width)


def solution(mesh):
    fine = Mesh(mesh.devices.reshape(4, 8, 4, 2), ("x", "z", "y", "c"))
    in_specs = (
        P(SEARCH, None, MP, None),
        P(SEARCH, None, None),
        P(SEARCH, None, None),
        P(SEARCH),
        P(MP, None, None),
        P(MP, None, None),
        P(MP, SEARCH),
        P(SEARCH, None, MP),
        P(MP, None),
        P(SEARCH, None, None),
        P(SEARCH, None, MP),
        P(SEARCH, None, MP),
        P(SEARCH, MP, None),
    )
    out_specs = P(SEARCH, None, MP)
    return jax.shard_map(local, mesh=fine, in_specs=in_specs, out_specs=out_specs, check_vma=False)
```

```python
import functools

import jax
import jax.numpy as jnp
from jax import lax
from jax.experimental import pallas as pl
from jax.experimental.layout import Layout, with_layout_constraint
from jax.experimental.pallas import tpu as pltpu
from jax.sharding import Mesh
from jax.sharding import PartitionSpec as P

D = 7168
SEARCH = ("x", "z")
MP = ("y", "c")
BF16 = jnp.bfloat16
F32 = jnp.float32


def exchange(values, axes):
    return lax.all_to_all(values, axes, split_axis=0, concat_axis=0, tiled=True)


def to_other_core(values):
    return lax.ppermute(values, "c", [(0, 1), (1, 0)])


def along_y(values, step):
    if step == 0:
        return values
    n = lax.axis_size("y")
    return lax.ppermute(values, "y", [(i, (i + step) % n) for i in range(n)])


def row_major(values):
    return with_layout_constraint(values, Layout(major_to_minor=tuple(range(values.ndim))))


def select_rows(matrix, rows):
    return jnp.dot(matrix, rows, preferred_element_type=F32).astype(BF16)


def attend_kernel(
    scale, chosen, arrived, up_keys, up_values, keys, out, packed, query, peak, mass, total
):
    children = chosen.shape[0]
    heads, nope_width, latent_width = up_keys.shape
    kv_width = keys.shape[0]
    rope_width = kv_width - latent_width
    steps = query.shape[0] // (heads * children)
    tokens = steps * children
    rope_from = heads * steps * nope_width
    keys_from = rope_from + heads * steps * rope_width
    key_stride = (arrived.shape[1] - keys_from) // steps
    dims = (((1,), (1,)), ((), ()))

    @pl.when(pl.program_id(0) == 0)
    def _():
        packed[...] = jnp.dot(
            chosen[...], arrived[...], preferred_element_type=F32
        ).astype(BF16)
        for h in range(heads):
            for t in range(steps):
                rows = pl.ds(h * tokens + t * children, children)
                block = h * steps + t
                query[rows, latent_width:] = packed[
                    :, rope_from + block * rope_width : rope_from + (block + 1) * rope_width
                ]
            at = h * steps * nope_width
            nope = jnp.concatenate(
                [packed[:, at + t * nope_width : at + (t + 1) * nope_width] for t in range(steps)], axis=0
            )
            query[pl.ds(h * tokens, tokens), :latent_width] = jnp.dot(
                nope, up_keys[h], preferred_element_type=F32
            ).astype(BF16)
        own = jnp.concatenate(
            [
                packed[:, keys_from + u * key_stride : keys_from + u * key_stride + kv_width]
                for u in range(steps)
            ],
            axis=0,
        )
        scores = lax.dot_general(query[...], own, dims, preferred_element_type=F32) * scale
        row = lax.rem(lax.broadcasted_iota(jnp.int32, scores.shape, 0), tokens)
        column = lax.broadcasted_iota(jnp.int32, scores.shape, 1)
        seen = (lax.rem(row, children) == lax.rem(column, children)) & (
            lax.div(column, children) <= lax.div(row, children)
        )
        scores = jnp.where(seen, scores, -1e30)
        top = jnp.max(scores, axis=1, keepdims=True)
        weights = jnp.where(seen, jnp.exp(scores - top), 0.0)
        peak[...] = jnp.broadcast_to(top, peak.shape)
        mass[...] = jnp.broadcast_to(jnp.sum(weights, axis=1, keepdims=True), mass.shape)
        total[...] = jnp.dot(
            weights.astype(BF16), own[:, :latent_width], preferred_element_type=F32
        )

    scores = jnp.dot(query[...], keys[...], preferred_element_type=F32) * scale
    before = peak[:, :1]
    top = jnp.maximum(before, jnp.max(scores, axis=1, keepdims=True))
    weights = jnp.exp(scores - top)
    shrink = jnp.exp(before - top)
    peak[...] = jnp.broadcast_to(top, peak.shape)
    mass[...] = mass[...] * shrink + jnp.sum(weights, axis=1, keepdims=True)
    total[...] = total[...] * shrink + lax.dot_general(
        weights.astype(BF16), keys[:latent_width, :], dims, preferred_element_type=F32
    )

    @pl.when(pl.program_id(0) == pl.num_programs(0) - 1)
    def _():
        value_width = up_values.shape[2]
        for h in range(heads):
            rows = pl.ds(h * tokens, tokens)
            latent_out = (total[rows, :] / mass[rows, :1]).astype(BF16)
            out[:, h * value_width : (h + 1) * value_width] = jnp.dot(
                latent_out, up_values[h], preferred_element_type=F32
            ).astype(BF16)


def attend(chosen, arrived, prefix, up_keys, up_values, steps, scale):
    children = chosen.shape[0]
    heads, _, latent_width = up_keys.shape
    value_width = up_values.shape[2]
    kv_width, prefix_len = prefix.shape
    rows = heads * steps * children
    key_block = prefix_len // 2
    whole = lambda array: pl.BlockSpec(array.shape, lambda i: (0,) * array.ndim)
    return pl.pallas_call(
        functools.partial(attend_kernel, scale),
        grid=(prefix_len // key_block,),
        in_specs=[
            whole(chosen),
            whole(arrived),
            whole(up_keys),
            whole(up_values),
            pl.BlockSpec((kv_width, key_block), lambda i: (0, i)),
        ],
        out_specs=pl.BlockSpec((steps * children, heads * value_width), lambda i: (0, 0)),
        out_shape=jax.ShapeDtypeStruct((steps * children, heads * value_width), BF16),
        scratch_shapes=[
            pltpu.VMEM((children, arrived.shape[1]), BF16),
            pltpu.VMEM((rows, kv_width), BF16),
            pltpu.VMEM((rows, 128), F32),
            pltpu.VMEM((rows, 128), F32),
            pltpu.VMEM((rows, latent_width), F32),
        ],
        compiler_params=pltpu.CompilerParams(vmem_limit_bytes=56 * 2**20),
        cost_estimate=pl.CostEstimate(
            flops=2 * rows * prefix_len * (kv_width + latent_width),
            bytes_accessed=2 * prefix_len * kv_width + 4 * up_keys.size,
            transcendentals=rows * prefix_len,
        ),
    )(chosen, arrived, up_keys, up_values, prefix)


def ring_gather(values, axis, due):
    n = lax.axis_size(axis)
    blocks = [None] * n
    blocks[0] = ahead = back = values
    for step in range(1, n // 2 + 1):
        ahead = lax.ppermute(ahead, axis, [(i, (i + 1) % n) for i in range(n)])
        if step == 2:
            ahead, due = lax.optimization_barrier((ahead, due))
        blocks[step] = ahead
        if step < n - step:
            back = lax.ppermute(back, axis, [(i, (i - 1) % n) for i in range(n)])
            blocks[n - step] = back
    return blocks, due


def cut_kernel(where, gate, up, down, *refs):
    *blocks, give, sems = refs
    n_y = len(blocks)
    rows, hidden = blocks[0].shape[0], gate.shape[2]
    units, width = down.shape[1], give.shape[1]
    copies = []
    for k, block in enumerate(blocks):
        to = lax.rem(where[0] + k, n_y)
        start = pl.multiple_of(to * rows, 128)
        column = pl.multiple_of((2 * to + 1 - where[1]) * width, 128)
        pieces = (
            (gate.at[0, pl.ds(start, rows), :], block.at[:, :hidden]),
            (up.at[0, pl.ds(start, rows), :], block.at[:, hidden:]),
            (down.at[0, :, pl.ds(column, width)], give.at[k * units : (k + 1) * units, :]),
        )
        for piece in pieces:
            copies.append(pltpu.make_async_copy(*piece, sems.at[len(copies)]))
            copies[-1].start()
    for copy in copies:
        copy.wait()


def cut(where, gate, up, down, n_y, width):
    away = pl.BlockSpec(memory_space=pl.ANY)
    block = jax.ShapeDtypeStruct((gate.shape[1] // n_y, 2 * gate.shape[2]), gate.dtype)
    give = jax.ShapeDtypeStruct((n_y * down.shape[1], width), down.dtype)
    *blocks, give = pl.pallas_call(
        cut_kernel,
        in_specs=[pl.BlockSpec(memory_space=pltpu.SMEM)] + [away] * 3,
        out_specs=[pl.BlockSpec(memory_space=pltpu.VMEM)] * (n_y + 1),
        out_shape=[block] * n_y + [give],
        scratch_shapes=[pltpu.SemaphoreType.DMA((3 * n_y,))],
        compiler_params=pltpu.CompilerParams(vmem_limit_bytes=56 * 2**20),
        cost_estimate=pl.CostEstimate(
            flops=0, bytes_accessed=4 * (gate.size + up.size) + 2 * down.size, transcendentals=0
        ),
    )(where, gate, up, down)
    return blocks, give


def project_kernel(where, *refs):
    *blocks, proj, keep, give, homes, rows = refs
    depth = proj.shape[2]
    each, per = keep.shape[2], blocks[0].shape[0]

    @pl.when(pl.program_id(0) == 0)
    def _():
        for k, block in enumerate(blocks):
            rows[k * per : (k + 1) * per, :] = block[:, :depth]
        top = jnp.concatenate([block[:16, depth:].astype(F32)[:1] for block in blocks], axis=0)
        half = len(blocks) // 2
        homes[...] = jnp.where(where[1] == 0, top[:half], top[half:])

    mine = rows[pl.ds(pl.multiple_of(where[1] * each, each), each), :]
    theirs = rows[pl.ds(pl.multiple_of((1 - where[1]) * each, each), each), :]
    dims = (((1,), (1,)), ((), ()))
    give[0] = lax.dot_general(proj[0], theirs, dims, preferred_element_type=F32).astype(BF16)
    keep[0] = lax.dot_general(proj[0], mine, dims, preferred_element_type=F32)


def project(where, blocks, proj):
    n_x, columns, depth = proj.shape
    rows = len(blocks) * blocks[0].shape[0]
    extra = blocks[0].shape[1] - depth
    out = (n_x, columns, rows // 2)
    step = pl.BlockSpec((1, columns, rows // 2), lambda k, where: (k, 0, 0))
    return pl.pallas_call(
        project_kernel,
        grid_spec=pltpu.PrefetchScalarGridSpec(
            num_scalar_prefetch=1,
            grid=(n_x,),
            in_specs=[pl.BlockSpec(block.shape, lambda k, where: (0, 0)) for block in blocks]
            + [
                pl.BlockSpec(
                    (1, columns, depth), lambda k, where: (lax.rem(where[0] + k, n_x), 0, 0)
                )
            ],
            out_specs=[
                step,
                step,
                pl.BlockSpec((len(blocks) // 2, extra), lambda k, where: (0, 0)),
            ],
            scratch_shapes=[pltpu.VMEM((rows, depth), BF16)],
        ),
        out_shape=[
            jax.ShapeDtypeStruct(out, F32),
            jax.ShapeDtypeStruct(out, BF16),
            jax.ShapeDtypeStruct((len(blocks) // 2, extra), F32),
        ],
        compiler_params=pltpu.CompilerParams(vmem_limit_bytes=56 * 2**20),
        cost_estimate=pl.CostEstimate(
            flops=2 * n_x * columns * depth * rows,
            bytes_accessed=2 * proj.size + 2 * rows * depth,
            transcendentals=0,
        ),
    )(where, *blocks, proj)


def land_kernel(core, picker, landed, keep, give):
    n_z = picker.shape[0]
    n_x = landed.shape[0] // n_z
    parts = []
    for z in range(n_z):
        rows = jnp.concatenate(
            [landed[x * n_z + z].astype(F32) for x in range(n_x)], axis=0
        ).astype(BF16)
        parts.append(jnp.dot(picker[z], rows, preferred_element_type=F32))
    low = jnp.concatenate(parts[: n_z // 2], axis=1)
    high = jnp.concatenate(parts[n_z // 2 :], axis=1)
    keep[...] = jnp.where(core[0] == 0, low, high)
    give[...] = jnp.where(core[0] == 0, high, low).astype(BF16)


def land(core, picker, landed):
    out = (picker.shape[1], picker.shape[0] // 2 * landed.shape[2])
    vmem = pl.BlockSpec(memory_space=pltpu.VMEM)
    return pl.pallas_call(
        land_kernel,
        in_specs=[pl.BlockSpec(memory_space=pltpu.SMEM), vmem, vmem],
        out_specs=[vmem] * 2,
        out_shape=[jax.ShapeDtypeStruct(out, F32), jax.ShapeDtypeStruct(out, BF16)],
        compiler_params=pltpu.CompilerParams(vmem_limit_bytes=8 * 2**20),
        cost_estimate=pl.CostEstimate(
            flops=2 * picker.size * landed.shape[2], bytes_accessed=4 * landed.size, transcendentals=0
        ),
    )(core.reshape(1), picker, landed)


def finish_kernel(own, other, *refs):
    *blocks, out = refs
    units = blocks[0].shape[0] // 2
    total = None
    for k, block in enumerate(blocks):
        span = slice(k * units, (k + 1) * units)
        part = jnp.dot(
            jnp.concatenate([own[:, span], other[:, span]], axis=1),
            block[...],
            preferred_element_type=F32,
        )
        total = part if total is None else total + part
    out[...] = total.astype(BF16)


def finish(own, other, blocks):
    vmem = pl.BlockSpec(memory_space=pltpu.VMEM)
    rows, columns = own.shape[0], blocks[0].shape[1]
    return pl.pallas_call(
        finish_kernel,
        in_specs=[vmem] * (2 + len(blocks)),
        out_specs=vmem,
        out_shape=jax.ShapeDtypeStruct((rows, columns), BF16),
        compiler_params=pltpu.CompilerParams(vmem_limit_bytes=14 * 2**20),
        cost_estimate=pl.CostEstimate(
            flops=4 * own.size * columns,
            bytes_accessed=4 * own.size + 2 * len(blocks) * blocks[0].size,
            transcendentals=0,
        ),
    )(own, other, *blocks)


def activate_kernel(count, core, rows, other, *refs):
    weights, rest = refs[:count], refs[count:]
    ride, outs = (rest[0], rest[1:]) if len(rest) > count else (None, rest)
    width = rows.shape[1]
    mine = pl.ds(pl.multiple_of(core[0] * width, 128), width)
    theirs = pl.ds(pl.multiple_of((1 - core[0]) * width, 128), width)
    for w, out in zip(weights, outs):
        act = jnp.dot(rows[...], w[mine, :], preferred_element_type=F32) + jnp.dot(
            other[...], w[theirs, :], preferred_element_type=F32
        )
        out[: rows.shape[0], :] = act.astype(out.dtype)
        if ride is not None:
            out[rows.shape[0] :, :] = ride[...]


def activate(core, rows, other, weights, ride=None):
    count, columns = len(weights), weights[0].shape[1]
    vmem = pl.BlockSpec(memory_space=pltpu.VMEM)
    if ride is None:
        shape = jax.ShapeDtypeStruct((rows.shape[0], columns), F32)
        operands = (rows, other, *weights)
    else:
        shape = jax.ShapeDtypeStruct((rows.shape[0] + ride.shape[0], columns), BF16)
        operands = (rows, other, *weights, ride)
    return pl.pallas_call(
        functools.partial(activate_kernel, count),
        in_specs=[pl.BlockSpec(memory_space=pltpu.SMEM)] + [vmem] * len(operands),
        out_specs=[vmem] * count,
        out_shape=[shape] * count,
        compiler_params=pltpu.CompilerParams(vmem_limit_bytes=12 * 2**20),
        cost_estimate=pl.CostEstimate(
            flops=4 * count * rows.size * columns,
            bytes_accessed=4 * rows.size + 2 * count * weights[0].size,
            transcendentals=0,
        ),
    )(core.reshape(1), *operands)


def local(
    queries,
    new_latents,
    parent_cache,
    parent_of,
    up_keys,
    up_values,
    out_proj,
    hidden_in,
    router,
    routes,
    w_gate,
    w_up,
    w_down,
):
    n_x, n_z, n_y, n_c = (lax.axis_size(a) for a in ("x", "z", "y", "c"))
    searchers = n_x * n_z
    children, steps, heads, query_width = queries.shape
    nope_width, latent_width = up_keys.shape[1:]
    rope_width = query_width - nope_width
    kv_width = parent_cache.shape[2]
    value_width = up_values.shape[2]
    tokens = children * steps
    width = hidden_in.shape[2]
    block = out_proj.shape[1]
    core = lax.axis_index("c")

    proj = lax.all_gather(out_proj.T, "x", axis=0, tiled=False)
    hidden_here = w_down.shape[1]
    here = lax.axis_index("y")
    place = jnp.stack([here, core]).astype(jnp.int32)
    gate_up, down_give = cut(place, w_gate, w_up, w_down, n_y, width)
    gate_up = [along_y(block_k, k) for k, block_k in enumerate(gate_up)]
    down_swapped = to_other_core(down_give)

    placer = (jnp.arange(searchers, dtype=jnp.int32)[:, None] == parent_of[None, :]).astype(BF16)
    nope = queries[..., :nope_width].transpose(0, 2, 1, 3).reshape(children, -1)
    rope = queries[..., nope_width:].transpose(0, 2, 1, 3).reshape(children, -1)
    fill = jnp.ones((children, steps, -kv_width % 128), BF16)
    keys = jnp.concatenate([new_latents, fill], axis=2).reshape(children, -1)
    payload = select_rows(placer, jnp.concatenate([nope, rope, keys], axis=1))
    arrived = exchange(payload.reshape(searchers, 2, -1), SEARCH).reshape(searchers, -1)

    present = arrived[:, -1].astype(F32)
    span = jnp.arange(searchers, dtype=jnp.int32)
    before = jnp.sum(jnp.where(span[None, :] < span[:, None], present[None, :], 0.0), axis=1)
    chosen = (
        (jnp.arange(children, dtype=F32)[:, None] == before[None, :]) & (present[None, :] > 0)
    ).astype(BF16)
    homes = jnp.sum(chosen.astype(F32) * span.astype(F32)[None, :], axis=1)
    attention = attend(
        chosen,
        arrived,
        parent_cache[0].T,
        up_keys,
        up_values,
        steps,
        float(query_width) ** (-0.5),
    )

    home_lanes = jnp.pad(jnp.tile(homes, steps), (0, -tokens % 128))
    home_rows = jnp.broadcast_to(home_lanes[None, :], (tokens, home_lanes.shape[0])).astype(BF16)
    attention = jnp.concatenate([attention, home_rows], axis=1)
    attention, down_swapped, routes, parent_of = lax.optimization_barrier(
        (attention, down_swapped, routes, parent_of)
    )
    gathered, proj = ring_gather(attention, "z", proj)
    keep, give, my_homes = project(place, gathered, proj)
    hidden_here = w_down.shape[1]
    down = []
    for k in range(n_y):
        start = (lax.rem(here + k, n_y) * n_c + core) * width
        own_k = lax.dynamic_slice_in_dim(w_down[0], start, width, axis=1)
        swapped_k = down_swapped[k * hidden_here : (k + 1) * hidden_here]
        down.append(jnp.concatenate([own_k, swapped_k], axis=0))
    experts = router.shape[1]
    topk = routes.shape[2]
    capacity = min(tokens, 3 * tokens * topk // (2 * experts))
    picked = routes.reshape(tokens, topk)
    named = jnp.any(
        picked[None, :, :] == jnp.arange(experts, dtype=jnp.int32)[:, None, None], axis=2
    )
    earlier = (
        jnp.arange(tokens, dtype=jnp.int32)[:, None] < jnp.arange(tokens, dtype=jnp.int32)[None, :]
    )
    rank = jnp.dot(named.astype(BF16), earlier.astype(BF16), preferred_element_type=F32)
    slot_of = (
        named[:, None, :]
        & (rank[:, None, :] == jnp.arange(capacity, dtype=F32)[None, :, None])
    ).reshape(experts * capacity, tokens)
    dispatcher = slot_of.astype(BF16)

    keep, give, gate_up, down, dispatcher = lax.optimization_barrier(
        (keep, give, gate_up, down, dispatcher)
    )

    paired = (keep + to_other_core(give).astype(F32)).astype(BF16)
    summed = sum(along_y(paired[k], k).astype(F32) for k in range(n_y)).astype(BF16)

    zs = n_z // n_c
    my_homes = my_homes[:, :tokens].reshape(-1)
    slot = jnp.arange(searchers * zs * steps, dtype=jnp.int32)
    row_at = jnp.arange(zs * tokens, dtype=jnp.int32)
    scatter = (
        my_homes.astype(jnp.int32)[None, :] == lax.div(slot, zs * steps)[:, None]
    ) & (lax.div(row_at, children)[None, :] == lax.rem(slot, zs * steps)[:, None])
    slots = lax.dot_general(
        scatter.astype(BF16), summed, (((1,), (1,)), ((), ())), preferred_element_type=F32
    ).astype(BF16)
    slots, down = lax.optimization_barrier((slots, down))
    down = [along_y(row_major(block_k), k) for k, block_k in enumerate(down)]
    landed = exchange(slots.reshape(searchers, zs * steps, block), SEARCH)
    sender = jnp.arange(n_z, dtype=jnp.int32)[:, None, None]
    parent_row = jnp.repeat(parent_of, steps)[None, :, None]
    step_row = lax.rem(jnp.arange(tokens, dtype=jnp.int32), steps)[None, :, None]
    column = jnp.arange(n_x * zs * steps, dtype=jnp.int32)[None, None, :]
    back = lax.rem(sender - lax.rem(parent_row, n_z) + n_z, n_z)
    picker = (
        (lax.div(parent_row, n_z) == lax.div(column, zs * steps))
        & (back == core * zs + lax.rem(lax.div(column, steps), zs))
        & (step_row == lax.rem(column, steps))
    ).astype(BF16)
    keep, give = land(core, picker, landed)
    projected = keep + to_other_core(give).astype(F32)
    residual = (hidden_in.reshape(tokens, width).astype(F32) + projected).astype(BF16)
    residual, down[1], down[3] = lax.optimization_barrier((residual, down[1], down[3]))
    residual_wide = residual.astype(F32)

    outgoing = lax.dot_general(
        dispatcher.reshape(-1, 4, tokens), residual, (((2,), (0,)), ((), ())), preferred_element_type=F32
    ).astype(BF16)
    quads = capacity // 4
    rows = exchange(outgoing.reshape(experts, quads, 4, width), SEARCH).reshape(
        experts * capacity, width
    )

    squares = jnp.sum(residual_wide * residual_wide, axis=1, keepdims=True)
    router_part = jnp.dot(residual, router, preferred_element_type=F32)
    stats = jnp.concatenate(
        [router_part, squares, jnp.zeros((tokens, 128 - experts - 1), F32)], axis=1
    )
    stats = stats + to_other_core(stats)
    stats = sum(along_y(stats, k) for k in range(n_y))
    stats, down = lax.optimization_barrier((stats, down))
    home_rms = lax.rsqrt(stats[:, experts] / D + 1e-06)
    affinity = jax.nn.sigmoid(stats[:, :experts] * home_rms[:, None])
    chosen_affinity = jnp.where(named.T, affinity, 0.0)
    gate_weight = 2.5 * chosen_affinity / jnp.sum(chosen_affinity, axis=1, keepdims=True)

    rows, gate_weight = lax.optimization_barrier((rows, gate_weight))
    other = to_other_core(rows)
    own_squares = jnp.sum(jnp.square(rows.astype(F32)), axis=1)
    row_squares = (own_squares + jnp.sum(jnp.square(other.astype(F32)), axis=1)).reshape(-1, 128)
    squares_top = row_squares.astype(BF16)
    squares_rest = (row_squares - squares_top.astype(F32)).astype(BF16)
    ride = jnp.concatenate([squares_top, squares_rest], axis=1)
    lines = ride.shape[0]
    ride = jnp.pad(ride, ((0, -lines % 16), (0, 0)))
    slots_total = experts * capacity
    partials = activate(core, rows, other, gate_up[1:], ride)
    arrivals = [along_y(partials[k - 1], n_y - k) for k in range(1, n_y)]
    [acts] = activate(core, rows, other, gate_up[:1])
    for arrival in arrivals:
        acts = acts + arrival[:slots_total].astype(F32)
        squares = arrival[slots_total : slots_total + lines].astype(F32)
        row_squares = row_squares + squares[:, :128] + squares[:, 128:]
    row_rms = lax.rsqrt(row_squares.reshape(-1) / D + 1e-06)
    acts = acts * row_rms[:, None]
    hidden = (jax.nn.silu(acts[:, :hidden_here]) * acts[:, hidden_here:]).astype(BF16)
    hidden_core = jnp.concatenate([along_y(hidden, k) for k in range(n_y)], axis=1)
    hidden_other = to_other_core(hidden_core)
    expert_out = finish(hidden_core, hidden_other, down)
    returned = exchange(expert_out.reshape(experts, quads, 4, width), SEARCH).reshape(
        experts * capacity, width
    )

    weight_of = jnp.where(
        slot_of.reshape(experts, capacity, tokens), gate_weight.T[:, None, :], 0.0
    ).reshape(experts * capacity, tokens)
    upper = weight_of.astype(BF16)
    lower = (weight_of - upper.astype(F32)).astype(BF16)
    dims = (((0,), (0,)), ((), ()))
    expert_mix = lax.dot_general(
        upper, returned, dims, preferred_element_type=F32
    ) + lax.dot_general(lower, returned, dims, preferred_element_type=F32)
    mixed = (residual_wide + expert_mix).astype(BF16)
    return mixed.reshape(children, steps, width)


def solution(mesh):
    fine = Mesh(mesh.devices.reshape(4, 8, 4, 2), ("x", "z", "y", "c"))
    in_specs = (
        P(SEARCH, None, MP, None),
        P(SEARCH, None, None),
        P(SEARCH, None, None),
        P(SEARCH),
        P(MP, None, None),
        P(MP, None, None),
        P(MP, SEARCH),
        P(SEARCH, None, MP),
        P(MP, None),
        P(SEARCH, None, None),
        P(SEARCH, None, MP),
        P(SEARCH, None, MP),
        P(SEARCH, MP, None),
    )
    out_specs = P(SEARCH, None, MP)
    return jax.shard_map(local, mesh=fine, in_specs=in_specs, out_specs=out_specs, check_vma=False)
```
